128 devices in a mesh: bin: 4 (over y_lo, core), tile: 32 (over z, x, y_hi).
Axes of the slice: x: 4, y: 4 (y_hi: 2, y_lo: 2; y = y_hi * 2 + y_lo), z: 4, core: 2. Of those that a mesh axis runs over, the one named last changes fastest.
Arguments:
- shear_one: float32 [4, 4096, 4096], P('bin', 'tile'), may hold values from -6 to 6
- shear_two: float32 [4, 4096, 4096], P('bin', 'tile'), may hold values from -6 to 6
- weights: float32 [4, 4], replicated, may hold values from 0.2 to 1
Outputs:
- convergence: float32 [4, 4096, 4096], P('bin', 'tile')
The draws below stay inside these ranges and needn't reach their ends.
All inputs are finite; a program needn't handle non-finite values.
Results may differ from the reference program's by a relative error of at most 0.000071.
Values sent between devices are 32-bit elements; how exact they have to be, the bound alone decides.
A program may use at most 128 MiB of HBM per device.

```python
import math
import jax
import jax.numpy as jnp
from jax import lax

N = 4096
BINS = 4


def steps_of(key, shape, pieces, smallest, high):
    level = 1.0
    for position, parts in pieces:
        heights = jax.random.uniform(jax.random.fold_in(jax.random.fold_in(key, 6), position), (parts,), jnp.float32, smallest / len(pieces), high / len(pieces))
        level = level * jnp.repeat(jnp.exp(heights), shape[position] // parts).reshape((-1,) + (1,) * (len(shape) - 1 - position))
    return level


def bell_draw(own_key, extent, spread, limit, pieces=(), kind=jnp.bfloat16):
    gain = steps_of(own_key, extent, pieces, -0.22, 0.18) if pieces else 1.0
    entries = jax.random.normal(own_key, extent, jnp.float32) * spread * gain
    return jnp.minimum(jnp.maximum(entries, -limit), limit).astype(kind)


def setup_inputs(seed: int = 0) -> dict:
    streams_of = jax.random.split(jax.random.key(seed), 4)
    shear_one = bell_draw(streams_of[0], (BINS, N, N), 1.0, 6.0, ((0, 4), (1, 32)), jnp.float32)
    shear_two = bell_draw(streams_of[1], (BINS, N, N), 1.0, 6.0, ((0, 4), (1, 32)), jnp.float32)
    weights = jnp.clip(jnp.exp(jax.random.uniform(streams_of[2], (BINS, BINS), jnp.float32, math.log(0.2), math.log(1.0))), 0.2, 1.0)
    return dict(shear_one=shear_one, shear_two=shear_two, weights=weights)


def signed_frequency(length):
    index = jnp.arange(length, dtype=jnp.int32)
    return jnp.where(index < length // 2, index, index - length)


def reference(shear_one, shear_two, weights):
    length = shear_one.shape[-1]
    frequency = signed_frequency(length)
    row_freq = frequency[:, None]
    col_freq = frequency[None, :]
    radius = col_freq * col_freq + row_freq * row_freq
    radius_floor = jnp.maximum(radius, 1).astype(jnp.float32)
    kern_real = (col_freq * col_freq - row_freq * row_freq).astype(jnp.float32) / radius_floor
    kern_imag = (2 * col_freq * row_freq).astype(jnp.float32) / radius_floor

    def convert(shears):
        spectrum = jnp.fft.fft2(lax.complex(shears[0], shears[1]))
        spec_real = jnp.real(spectrum)
        spec_imag = jnp.imag(spectrum)
        new_real = kern_real * spec_real + kern_imag * spec_imag
        new_imag = kern_real * spec_imag - kern_imag * spec_real
        return jnp.real(jnp.fft.ifft2(lax.complex(new_real, new_imag)))

    fields = lax.map(convert, (shear_one, shear_two))
    order_index = jnp.arange(weights.shape[0], dtype=jnp.int32)
    masked = jnp.where(order_index[:, None] >= order_index[None, :], weights, jnp.zeros_like(weights))
    return jnp.einsum("ji,irc->jrc", masked, fields, precision=lax.Precision.HIGHEST)
```

```python
import functools

import jax
import jax.numpy as jnp
import ml_dtypes
import numpy as np
from jax import lax
from jax.experimental import pallas as pl
from jax.experimental.pallas import tpu as pltpu
from jax.sharding import PartitionSpec as P

N = 4096
A = 32
L = 128
DEV = 128
BINS = 4
F32 = jnp.float32
BF16 = jnp.bfloat16


def hi_lo(matrix):
    hi = matrix.astype(ml_dtypes.bfloat16)
    lo = (matrix - hi.astype(np.float64)).astype(ml_dtypes.bfloat16)
    return np.stack([hi, lo])


def tables():
    lane = np.arange(L)
    angle = 2.0 * np.pi * ((lane[:, None] * lane[None, :]) % L) / L
    c, s = np.cos(angle), np.sin(angle)
    fwd = np.block([[c, s], [-s, c]])
    slot = np.arange(64)
    a0 = 2.0 * np.pi * ((slot[:, None] * lane[None, :]) % L) / L
    a16 = 2.0 * np.pi * (((16 + 32 * slot[:, None]) * lane[None, :]) % N) / N
    first = np.zeros((256, 256))
    first[0:64, 0:128] = np.cos(a0)
    first[128:192, 0:128] = -np.sin(a0)
    first[128, 0:128] = (-1.0) ** lane
    first[64:128, 128:256] = np.cos(a16)
    first[192:256, 128:256] = -np.sin(a16)
    last = 2.0 * first.copy()
    last[0, 0:128] = 1.0
    last[128, 0:128] = (-1.0) ** lane
    k = np.arange(A)
    tw = 2.0 * np.pi * ((k[:, None] * lane[None, :]) % N) / N
    twid = np.stack([np.cos(tw), np.sin(tw)], 1).astype(np.float32)
    twid = np.broadcast_to(twid[:, :, None, :], (A, 2, 8, L)).copy()
    return dict(
        row=np.stack([hi_lo(first), hi_lo(fwd)]),
        colf=hi_lo(fwd.T),
        coli=hi_lo(fwd),
        back=np.stack([hi_lo(last), hi_lo(fwd)]),
        twid=twid,
    )


def fft(xs, sign):
    n = len(xs)
    if n == 1:
        return xs
    even, odd = fft(xs[0::2], sign), fft(xs[1::2], sign)
    out = [None] * n
    h = n // 2
    root = np.float32(np.sqrt(0.5))
    for k in range(h):
        er, ei = even[k]
        r, i = odd[k]
        if k == 0:
            tr, ti = r, i
        elif 4 * k == n:
            tr, ti = (-i, r) if sign > 0 else (i, -r)
            if sign > 0:
                out[k], out[k + h] = (er - i, ei + r), (er + i, ei - r)
            else:
                out[k], out[k + h] = (er + i, ei - r), (er - i, ei + r)
            continue
        elif 8 * k == n:
            tr, ti = ((r - i) * root, (r + i) * root) if sign > 0 else ((r + i) * root, (i - r) * root)
        elif 8 * k == 3 * n:
            if sign > 0:
                pr, pi = (r + i) * root, (r - i) * root
                out[k], out[k + h] = (er - pr, ei + pi), (er + pr, ei - pi)
            else:
                pr, pi = (i - r) * root, (r + i) * root
                out[k], out[k + h] = (er + pr, ei - pi), (er - pr, ei + pi)
            continue
        else:
            c = np.float32(np.cos(2 * np.pi * k / n))
            s = np.float32(sign * np.sin(2 * np.pi * k / n))
            tr, ti = r * c - i * s, r * s + i * c
        out[k], out[k + h] = (er + tr, ei + ti), (er - tr, ei - ti)
    return out


def rfft(xs):
    n = len(xs)
    if n == 2:
        return [(xs[0] + xs[1], None), (xs[0] - xs[1], None)]
    even, odd = rfft(xs[0::2]), rfft(xs[1::2])
    out = [None] * (n // 2 + 1)
    for k in range(n // 4 + 1):
        if k == 0:
            out[0] = (even[0][0] + odd[0][0], None)
            out[n // 2] = (even[0][0] - odd[0][0], None)
        elif 4 * k == n:
            out[k] = (even[k][0], -odd[k][0])
        else:
            er, ei = even[k]
            r, i = odd[k]
            if 8 * k == n:
                root = np.float32(np.sqrt(0.5))
                tr, ti = (r + i) * root, (i - r) * root
            else:
                c = np.float32(np.cos(2 * np.pi * k / n))
                s = np.float32(np.sin(2 * np.pi * k / n))
                tr, ti = r * c + i * s, i * c - r * s
            out[k] = (er + tr, ei + ti)
            out[n // 2 - k] = (er - tr, ti - ei)
    return out


def irfft(X, n):
    if n == 2:
        a, b = X[0][0], X[1][0]
        return [a + b, a - b]
    h = n // 2
    even, odd = [None] * (h // 2 + 1), [None] * (h // 2 + 1)
    for k in range(h // 2 + 1):
        if k == 0:
            even[0] = (X[0][0] + X[h][0], None)
            odd[0] = (X[0][0] - X[h][0], None)
        elif 2 * k == h:
            even[k] = (X[k][0] + X[k][0], None)
            odd[k] = (-(X[k][1] + X[k][1]), None)
        else:
            ar, ai = X[k]
            br, bi = X[h - k]
            even[k] = (ar + br, ai - bi)
            dr, di = ar - br, ai + bi
            if 4 * k == h:
                root = np.float32(np.sqrt(0.5))
                odd[k] = ((dr - di) * root, (dr + di) * root)
            else:
                c = np.float32(np.cos(2 * np.pi * k / n))
                s = np.float32(np.sin(2 * np.pi * k / n))
                odd[k] = (dr * c - di * s, dr * s + di * c)
    e, o = irfft(even, h), irfft(odd, h)
    out = [None] * n
    out[0::2] = e
    out[1::2] = o
    return out


def split(x):
    hi = x.astype(BF16)
    lo = (x - hi.astype(F32)).astype(BF16)
    return hi, lo


ROWS = 16
STEPS = 128 // ROWS


def row_kernel(g1_ref, g2_ref, tw_ref, w_ref, *refs):
    outs, y_ref = refs[:-1], refs[-1]
    i = pl.program_id(0)

    @pl.when(i < STEPS)
    def _():
        for comp, g_ref in enumerate((g1_ref, g2_ref)):
            for j in range(ROWS // 8):
                xs = [g_ref[8 * j : 8 * j + 8, L * p : L * p + L] for p in range(A)]
                X = rfft(xs)
                rows = pl.ds(pl.multiple_of(128 * comp + i * ROWS + 8 * j, 8), 8)
                y_ref[0, rows, 0:L] = X[0][0]
                y_ref[0, rows, L : 2 * L] = X[16][0]
                for k in range(1, 16):
                    r, m = X[k]
                    c, s = tw_ref[k, 0], tw_ref[k, 1]
                    y_ref[k, rows, 0:L] = r * c + m * s
                    y_ref[k, rows, L : 2 * L] = m * c - r * s

    @pl.when(i >= STEPS)
    def _():
        k = i - STEPS
        hi, lo = split(y_ref[k])
        sel = jnp.minimum(k, 1)
        whi, wlo = w_ref[sel, 0], w_ref[sel, 1]
        dims = (((1,), (1,)), ((), ()))
        dot = functools.partial(lax.dot_general, dimension_numbers=dims, preferred_element_type=F32)
        out = dot(whi, hi) + (dot(whi, lo) + dot(wlo, hi))
        for h in range(2):
            for c in range(2):
                for d in range(8):
                    at = 128 * c + 64 * h + 8 * d
                    outs[h][d, c] = out[at : at + 8]


def row_stage(g1, g2, tab):
    g1, g2 = g1.reshape(128, N), g2.reshape(128, N)
    last = STEPS - 1
    return pl.pallas_call(
        row_kernel,
        grid=(STEPS + 16,),
        in_specs=[
            pl.BlockSpec((ROWS, N), lambda i: (jnp.minimum(i, last), 0)),
            pl.BlockSpec((ROWS, N), lambda i: (jnp.minimum(i, last), 0)),
            pl.BlockSpec((A, 2, 8, L), lambda i: (0, 0, 0, 0)),
            pl.BlockSpec((2, 2, 256, 256), lambda i: (0, 0, 0, 0)),
        ],
        out_specs=[pl.BlockSpec((8, 2, 8, 256), lambda i: (jnp.maximum(i - STEPS, 0), 0, 0, 0))] * 2,
        out_shape=[jax.ShapeDtypeStruct((DEV, 2, 8, 256), F32)] * 2,
        scratch_shapes=[pltpu.VMEM((16, 256, 256), F32)],
        cost_estimate=pl.CostEstimate(flops=10**9, bytes_accessed=8 * 2**20, transcendentals=0),
        name="rows",
    )(g1, g2, tab["twid"], tab["row"])


GROUP = 4


def col_kernel(half, wgt_ref, x_ref, tw_ref, wf_ref, wi_ref, out_ref, y_ref, z_ref):
    i = pl.program_id(0)
    dev = lax.axis_index(("bin", "tile"))
    group, part = dev // 8, dev % 8
    sub = lax.broadcasted_iota(jnp.int32, (8, L), 0)
    lane = lax.broadcasted_iota(jnp.int32, (8, L), 1)
    if half == 0:
        packed = jnp.logical_and(sub == 0, dev == 0)

    @pl.when(i < BINS)
    def _():
        if half == 0:
            sign = jnp.where(lane % 2 == 0, 1.0, -1.0).astype(F32)
            total = x_ref[0, 1, :, L : 2 * L]
            for t in range(1, A):
                total = total + x_ref[t, 1, :, L : 2 * L]
            corner = sign * (jnp.sum(total * sign, axis=1, keepdims=True) * np.float32(-1.0 / N))
        for R in range(2):
            xs = []
            for t in range(A):
                re = x_ref[t, 0, :, R * L : R * L + L]
                im = x_ref[t, 1, :, R * L : R * L + L]
                if half == 0:
                    if R == 0:
                        im = jnp.where(packed, corner, im)
                    else:
                        re = jnp.where(packed, 0.0, re)
                        im = jnp.where(packed, x_ref[t, 1, :, 0:L], im)
                xs.append((re, im))
            X = fft(xs, -1)
            rows = pl.ds(pl.multiple_of(32 * R + 8 * i, 8), 8)
            for k in range(A):
                r, m = X[k]
                if k:
                    c, s = tw_ref[k, 0], tw_ref[k, 1]
                    r, m = r * c + m * s, m * c - r * s
                y_ref[k, rows, 0:L] = r
                y_ref[k, rows, L : 2 * L] = m

    @pl.when(jnp.logical_and(i >= BINS, i < BINS + A // GROUP))
    def _():
        base = (i - BINS) * GROUP
        hi, lo = split(y_ref[pl.ds(base, GROUP)].reshape(GROUP * 64, 256))
        dot = functools.partial(jnp.dot, preferred_element_type=F32)
        G = dot(hi, wf_ref[0]) + (dot(lo, wf_ref[0]) + dot(hi, wf_ref[1]))
        at = 8 * part + sub
        col = jnp.where(group == 0, 32 * at + 16 * half, group + 32 * (64 * half + at))
        col = jnp.where(col < N // 2, col, col - N).astype(F32)
        scale = np.float32(1.0 / (N * N))
        w = [[wgt_ref[j, b] * scale for b in range(j + 1)] for j in range(BINS)]
        rows = []
        for kk in range(GROUP):
            u = base + kk + A * lane
            nyquist = u == N // 2
            row = jnp.where(u < N // 2, u, u - N).astype(F32)
            row2 = row * row

            def kern(l1):
                q = jnp.maximum(l1 * l1 + row2, 1.0)
                return (l1 * l1 - row2) / q, (2.0 * l1) * row / q

            a, b = kern(col)
            ar, ai = a, jnp.where(nyquist, -b, 0.0)
            br = jnp.where(nyquist, 0.0, b)
            if half == 0:
                a2, b2 = kern(jnp.full_like(col, -N // 2))
                br = jnp.where(packed, a2, br)
                bi = jnp.where(jnp.logical_and(packed, jnp.logical_not(nyquist)), -b2, 0.0)
            H = []
            for b_ in range(BINS):
                o1, o2 = kk * 64 + 8 * b_, kk * 64 + 32 + 8 * b_
                g1r, g1i = G[o1 : o1 + 8, 0:L], G[o1 : o1 + 8, L : 2 * L]
                g2r, g2i = G[o2 : o2 + 8, 0:L], G[o2 : o2 + 8, L : 2 * L]
                hr = ar * g1r - ai * g1i + br * g2r
                hm = ar * g1i + ai * g1r + br * g2i
                if half == 0:
                    hr, hm = hr - bi * g2i, hm + bi * g2r
                H.append((hr, hm))
            for j in range(BINS):
                fr, fi = H[0][0] * w[j][0], H[0][1] * w[j][0]
                for b_ in range(1, j + 1):
                    fr, fi = fr + H[b_][0] * w[j][b_], fi + H[b_][1] * w[j][b_]
                rows.append(jnp.concatenate([fr, fi], axis=1))
        hi, lo = split(jnp.concatenate(rows, axis=0))
        Z = dot(hi, wi_ref[0]) + (dot(lo, wi_ref[0]) + dot(hi, wi_ref[1]))
        for kk in range(GROUP):
            c, s = tw_ref[base + kk, 0], tw_ref[base + kk, 1]
            for j in range(BINS):
                o = 32 * kk + 8 * j
                r, m = Z[o : o + 8, 0:L], Z[o : o + 8, L : 2 * L]
                z_ref[base + kk, 8 * j : 8 * j + 8, 0:L] = r * c - m * s
                z_ref[base + kk, 8 * j : 8 * j + 8, L : 2 * L] = m * c + r * s

    @pl.when(i >= BINS + A // GROUP)
    def _():
        j = i - (BINS + A // GROUP)
        rows = pl.ds(pl.multiple_of(8 * j, 8), 8)
        xs = [(z_ref[k, rows, 0:L], z_ref[k, rows, L : 2 * L]) for k in range(A)]
        for t, (r, m) in enumerate(fft(xs, 1)):
            out_ref[t, 0] = r
            out_ref[t, 1] = m


def col_stage(x, weights, tab, half):
    before = BINS + A // GROUP
    return pl.pallas_call(
        functools.partial(col_kernel, half),
        grid=(before + BINS,),
        in_specs=[
            pl.BlockSpec(memory_space=pltpu.SMEM),
            pl.BlockSpec((A, 2, 8, 256), lambda i: (jnp.minimum(i, BINS - 1), 0, 0, 0)),
            pl.BlockSpec((A, 2, 8, L), lambda i: (0, 0, 0, 0)),
            pl.BlockSpec((2, 256, 256), lambda i: (0, 0, 0)),
            pl.BlockSpec((2, 256, 256), lambda i: (0, 0, 0)),
        ],
        out_specs=pl.BlockSpec((A, 2, 8, L), lambda i: (jnp.maximum(i - before, 0), 0, 0, 0)),
        out_shape=jax.ShapeDtypeStruct((DEV, 2, 8, L), F32),
        scratch_shapes=[pltpu.VMEM((A, 64, 256), F32), pltpu.VMEM((A, 32, 256), F32)],
        cost_estimate=pl.CostEstimate(flops=10**9, bytes_accessed=4 * 2**20, transcendentals=0),
        name="cols%d" % half,
    )(weights, x, tab["twid"], tab["colf"], tab["coli"])


def back_kernel(x0_ref, x1_ref, tw_ref, w_ref, out_ref, z_ref):
    i = pl.program_id(0)

    @pl.when(i < 16)
    def _():
        parts = []
        for c in range(2):
            for ref in (x0_ref, x1_ref):
                for d in range(8):
                    parts.append(ref[d, c])
        hi, lo = split(jnp.concatenate(parts, axis=0).T)
        sel = jnp.minimum(i, 1)
        dot = functools.partial(jnp.dot, preferred_element_type=F32)
        Z = dot(hi, w_ref[sel, 0]) + (dot(lo, w_ref[sel, 0]) + dot(hi, w_ref[sel, 1]))
        c, s = tw_ref[i, 0, 0:1], tw_ref[i, 1, 0:1]
        r, m = Z[:, 0:L], Z[:, L : 2 * L]
        z_ref[i, :, 0:L] = r * c - m * s
        z_ref[i, :, L : 2 * L] = m * c + r * s

    @pl.when(i >= 16)
    def _():
        for j in range(ROWS // 8):
            rows = pl.ds(pl.multiple_of((i - 16) * ROWS + 8 * j, 8), 8)
            X = [(z_ref[0, rows, 0:L], None)]
            X += [(z_ref[k, rows, 0:L], z_ref[k, rows, L : 2 * L]) for k in range(1, 16)]
            X += [(z_ref[0, rows, L : 2 * L], None)]
            for p, v in enumerate(irfft(X, A)):
                out_ref[8 * j : 8 * j + 8, L * p : L * p + L] = v


def back_stage(x0, x1, tab):
    return pl.pallas_call(
        back_kernel,
        grid=(16 + STEPS,),
        in_specs=[
            pl.BlockSpec((8, 2, 8, L), lambda i: (jnp.minimum(i, 15), 0, 0, 0)),
            pl.BlockSpec((8, 2, 8, L), lambda i: (jnp.minimum(i, 15), 0, 0, 0)),
            pl.BlockSpec((A, 2, 8, L), lambda i: (0, 0, 0, 0)),
            pl.BlockSpec((2, 2, 256, 256), lambda i: (0, 0, 0, 0)),
        ],
        out_specs=pl.BlockSpec((ROWS, N), lambda i: (jnp.maximum(i - 16, 0), 0)),
        out_shape=jax.ShapeDtypeStruct((128, N), F32),
        scratch_shapes=[pltpu.VMEM((16, 128, 256), F32)],
        cost_estimate=pl.CostEstimate(flops=10**9, bytes_accessed=4 * 2**20, transcendentals=0),
        name="back",
    )(x0, x1, tab["twid"], tab["back"])


def exchange(x):
    return lax.all_to_all(x, ("bin", "tile"), split_axis=0, concat_axis=0, tiled=True)


def on_device(shear_one, shear_two, weights):
    tab = {k: jnp.asarray(v) for k, v in tables().items()}
    halves = row_stage(shear_one, shear_two, tab)
    back = []
    for half in range(2):
        got = exchange(halves[half])
        back.append(exchange(col_stage(got, weights, tab, half)))
    return back_stage(back[0], back[1], tab).reshape(1, 128, N)


def solution(mesh):
    spec = P("bin", "tile", None)
    return jax.shard_map(
        on_device, mesh=mesh, in_specs=(spec, spec, P()), out_specs=spec, check_vma=False
    )
```

```python
import functools

import jax
import jax.numpy as jnp
import ml_dtypes
import numpy as np
from jax import lax
from jax.experimental import pallas as pl
from jax.experimental.pallas import tpu as pltpu
from jax.sharding import PartitionSpec as P

N = 4096
A = 32
L = 128
DEV = 128
BINS = 4
F32 = jnp.float32
BF16 = jnp.bfloat16


def hi_lo(matrix):
    hi = matrix.astype(ml_dtypes.bfloat16)
    lo = (matrix - hi.astype(np.float64)).astype(ml_dtypes.bfloat16)
    return np.stack([hi, lo])


def tables():
    lane = np.arange(L)
    angle = 2.0 * np.pi * ((lane[:, None] * lane[None, :]) % L) / L
    c, s = np.cos(angle), np.sin(angle)
    fwd = np.block([[c, s], [-s, c]])
    slot = np.arange(64)
    a0 = 2.0 * np.pi * ((slot[:, None] * lane[None, :]) % L) / L
    a16 = 2.0 * np.pi * (((16 + 32 * slot[:, None]) * lane[None, :]) % N) / N
    first = np.zeros((256, 256))
    first[0:64, 0:128] = np.cos(a0)
    first[128:192, 0:128] = -np.sin(a0)
    first[128, 0:128] = (-1.0) ** lane
    first[64:128, 128:256] = np.cos(a16)
    first[192:256, 128:256] = -np.sin(a16)
    last = 2.0 * first.copy()
    last[0, 0:128] = 1.0
    last[128, 0:128] = (-1.0) ** lane
    k = np.arange(A)
    tw = 2.0 * np.pi * ((k[:, None] * lane[None, :]) % N) / N
    twid = np.stack([np.cos(tw), np.sin(tw)], 1).astype(np.float32)
    twid = np.broadcast_to(twid[:, :, None, :], (A, 2, 8, L)).copy()
    return dict(
        row=np.stack([hi_lo(first), hi_lo(fwd)]),
        colf=hi_lo(fwd.T),
        coli=hi_lo(fwd),
        back=np.stack([hi_lo(last), hi_lo(fwd)]),
        twid=twid,
    )


def fft(xs, sign):
    n = len(xs)
    if n == 1:
        return xs
    even, odd = fft(xs[0::2], sign), fft(xs[1::2], sign)
    out = [None] * n
    h = n // 2
    root = np.float32(np.sqrt(0.5))
    for k in range(h):
        er, ei = even[k]
        r, i = odd[k]
        if k == 0:
            tr, ti = r, i
        elif 4 * k == n:
            tr, ti = (-i, r) if sign > 0 else (i, -r)
            if sign > 0:
                out[k], out[k + h] = (er - i, ei + r), (er + i, ei - r)
            else:
                out[k], out[k + h] = (er + i, ei - r), (er - i, ei + r)
            continue
        elif 8 * k == n:
            tr, ti = ((r - i) * root, (r + i) * root) if sign > 0 else ((r + i) * root, (i - r) * root)
        elif 8 * k == 3 * n:
            if sign > 0:
                pr, pi = (r + i) * root, (r - i) * root
                out[k], out[k + h] = (er - pr, ei + pi), (er + pr, ei - pi)
            else:
                pr, pi = (i - r) * root, (r + i) * root
                out[k], out[k + h] = (er + pr, ei - pi), (er - pr, ei + pi)
            continue
        else:
            c = np.float32(np.cos(2 * np.pi * k / n))
            s = np.float32(sign * np.sin(2 * np.pi * k / n))
            tr, ti = r * c - i * s, r * s + i * c
        out[k], out[k + h] = (er + tr, ei + ti), (er - tr, ei - ti)
    return out


def rfft(xs):
    n = len(xs)
    if n == 2:
        return [(xs[0] + xs[1], None), (xs[0] - xs[1], None)]
    even, odd = rfft(xs[0::2]), rfft(xs[1::2])
    out = [None] * (n // 2 + 1)
    for k in range(n // 4 + 1):
        if k == 0:
            out[0] = (even[0][0] + odd[0][0], None)
            out[n // 2] = (even[0][0] - odd[0][0], None)
        elif 4 * k == n:
            out[k] = (even[k][0], -odd[k][0])
        else:
            er, ei = even[k]
            r, i = odd[k]
            if 8 * k == n:
                root = np.float32(np.sqrt(0.5))
                tr, ti = (r + i) * root, (i - r) * root
            else:
                c = np.float32(np.cos(2 * np.pi * k / n))
                s = np.float32(np.sin(2 * np.pi * k / n))
                tr, ti = r * c + i * s, i * c - r * s
            out[k] = (er + tr, ei + ti)
            out[n // 2 - k] = (er - tr, ti - ei)
    return out


def irfft(X, n):
    if n == 2:
        a, b = X[0][0], X[1][0]
        return [a + b, a - b]
    h = n // 2
    even, odd = [None] * (h // 2 + 1), [None] * (h // 2 + 1)
    for k in range(h // 2 + 1):
        if k == 0:
            even[0] = (X[0][0] + X[h][0], None)
            odd[0] = (X[0][0] - X[h][0], None)
        elif 2 * k == h:
            even[k] = (X[k][0] + X[k][0], None)
            odd[k] = (-(X[k][1] + X[k][1]), None)
        else:
            ar, ai = X[k]
            br, bi = X[h - k]
            even[k] = (ar + br, ai - bi)
            dr, di = ar - br, ai + bi
            if 4 * k == h:
                root = np.float32(np.sqrt(0.5))
                odd[k] = ((dr - di) * root, (dr + di) * root)
            else:
                c = np.float32(np.cos(2 * np.pi * k / n))
                s = np.float32(np.sin(2 * np.pi * k / n))
                odd[k] = (dr * c - di * s, dr * s + di * c)
    e, o = irfft(even, h), irfft(odd, h)
    out = [None] * n
    out[0::2] = e
    out[1::2] = o
    return out


def split(x):
    hi = x.astype(BF16)
    lo = (x - hi.astype(F32)).astype(BF16)
    return hi, lo


ROWS = 16
STEPS = 128 // ROWS
GROUP = 4
MESH = pl.DeviceIdType.MESH


def mesh_id(device):
    return (device // 32, device % 32)


def row_butterflies(i, x_ref, tw_ref, y_ref):
    for comp in range(2):
        at = pl.ds(pl.multiple_of(8 * i, 8), 8)
        X = rfft([x_ref[comp, at, L * p : L * p + L] for p in range(A)])
        rows = pl.ds(pl.multiple_of(128 * comp + 8 * i, 8), 8)
        y_ref[0, rows, 0:L] = X[0][0]
        y_ref[0, rows, L : 2 * L] = X[16][0]
        for k in range(1, 16):
            r, m = X[k]
            c, s = tw_ref[k, 0], tw_ref[k, 1]
            y_ref[k, rows, 0:L] = r * c + m * s
            y_ref[k, rows, L : 2 * L] = m * c - r * s


def row_matmul(k, w_ref, y_ref, send_ref):
    hi, lo = split(y_ref[k])
    sel = jnp.minimum(k, 1)
    whi, wlo = w_ref[sel, 0], w_ref[sel, 1]
    dims = (((1,), (1,)), ((), ()))
    dot = functools.partial(lax.dot_general, dimension_numbers=dims, preferred_element_type=F32)
    out = dot(whi, hi) + (dot(whi, lo) + dot(wlo, hi))
    for h in range(2):
        for c in range(2):
            for d in range(8):
                at = 128 * c + 64 * h + 8 * d
                send_ref[h, 8 * k + d, c] = out[at : at + 8]


def col_forward(half, b, packed, x_ref, tw_ref, y_ref):
    lane = lax.broadcasted_iota(jnp.int32, (8, L), 1)
    sign = jnp.where(lane % 2 == 0, 1.0, -1.0).astype(F32)
    total = x_ref[half, A * b, 1, :, L : 2 * L]
    for t in range(1, A):
        total = total + x_ref[half, A * b + t, 1, :, L : 2 * L]
    corner = sign * (jnp.sum(total * sign, axis=1, keepdims=True) * np.float32(-1.0 / N))
    for R in range(2):
        xs = []
        for t in range(A):
            re = x_ref[half, A * b + t, 0, :, R * L : R * L + L]
            im = x_ref[half, A * b + t, 1, :, R * L : R * L + L]
            if R == 0:
                im = jnp.where(packed, corner, im)
            else:
                re = jnp.where(packed, 0.0, re)
                im = jnp.where(packed, x_ref[half, A * b + t, 1, :, 0:L], im)
            xs.append((re, im))
        X = fft(xs, -1)
        rows = pl.ds(pl.multiple_of(32 * R + 8 * b, 8), 8)
        for k in range(A):
            r, m = X[k]
            if k:
                c, s = tw_ref[k, 0], tw_ref[k, 1]
                r, m = r * c + m * s, m * c - r * s
            y_ref[k, rows, 0:L] = r
            y_ref[k, rows, L : 2 * L] = m


def col_middle(half, g, me, packed, w, tw_ref, wf_ref, wi_ref, y_ref, z_ref):
    base = g * GROUP
    group, part = me // 8, me % 8
    sub = lax.broadcasted_iota(jnp.int32, (8, L), 0)
    lane = lax.broadcasted_iota(jnp.int32, (8, L), 1)
    hi, lo = split(y_ref[pl.ds(base, GROUP)].reshape(GROUP * 64, 256))
    dot = functools.partial(jnp.dot, preferred_element_type=F32)
    G = dot(hi, wf_ref[0]) + (dot(lo, wf_ref[0]) + dot(hi, wf_ref[1]))
    at = 8 * part + sub
    col = jnp.where(group == 0, 32 * at + 16 * half, group + 32 * (64 * half + at))
    col = jnp.where(col < N // 2, col, col - N).astype(F32)
    rows = []
    for kk in range(GROUP):
        u = base + kk + A * lane
        nyquist = u == N // 2
        row = jnp.where(u < N // 2, u, u - N).astype(F32)
        row2 = row * row

        def kern(l1):
            q = jnp.maximum(l1 * l1 + row2, 1.0)
            return (l1 * l1 - row2) / q, (2.0 * l1) * row / q

        a, b = kern(col)
        ar, ai = a, jnp.where(nyquist, -b, 0.0)
        a2, b2 = kern(np.float32(-N // 2))
        br = jnp.where(packed, a2, jnp.where(nyquist, 0.0, b))
        bi = jnp.where(jnp.logical_and(packed, jnp.logical_not(nyquist)), -b2, 0.0)
        H = []
        for b_ in range(BINS):
            o1, o2 = kk * 64 + 8 * b_, kk * 64 + 32 + 8 * b_
            g1r, g1i = G[o1 : o1 + 8, 0:L], G[o1 : o1 + 8, L : 2 * L]
            g2r, g2i = G[o2 : o2 + 8, 0:L], G[o2 : o2 + 8, L : 2 * L]
            hr = ar * g1r - ai * g1i + br * g2r - bi * g2i
            hm = ar * g1i + ai * g1r + br * g2i + bi * g2r
            H.append((hr, hm))
        for j in range(BINS):
            fr, fi = H[0][0] * w[j][0], H[0][1] * w[j][0]
            for b_ in range(1, j + 1):
                fr, fi = fr + H[b_][0] * w[j][b_], fi + H[b_][1] * w[j][b_]
            rows.append(jnp.concatenate([fr, fi], axis=1))
    hi, lo = split(jnp.concatenate(rows, axis=0))
    Z = dot(hi, wi_ref[0]) + (dot(lo, wi_ref[0]) + dot(hi, wi_ref[1]))
    for kk in range(GROUP):
        c, s = tw_ref[base + kk, 0], tw_ref[base + kk, 1]
        for j in range(BINS):
            o = 32 * kk + 8 * j
            r, m = Z[o : o + 8, 0:L], Z[o : o + 8, L : 2 * L]
            z_ref[base + kk, 8 * j : 8 * j + 8, 0:L] = r * c - m * s
            z_ref[base + kk, 8 * j : 8 * j + 8, L : 2 * L] = m * c + r * s


def col_inverse(half, j, z_ref, ret_ref):
    rows = pl.ds(pl.multiple_of(8 * j, 8), 8)
    xs = [(z_ref[k, rows, 0:L], z_ref[k, rows, L : 2 * L]) for k in range(A)]
    for t, (r, m) in enumerate(fft(xs, 1)):
        ret_ref[half, A * j + t, 0] = r
        ret_ref[half, A * j + t, 1] = m


def main_kernel(
    wgt_ref, g1_ref, g2_ref, tw_ref, wr_ref, wf_ref, wi_ref, out_ref,
    x_ref, yr_ref, send_ref, recv_ref, y_ref, z_ref, ret_ref,
    in_sem, go_send, go_recv, ret_send, ret_recv, own_sem,
):
    me = lax.axis_index("bin") * 32 + lax.axis_index("tile")

    barrier = pltpu.get_barrier_semaphore()

    def greet(i, carry):
        pl.semaphore_signal(
            barrier, inc=1, device_id=mesh_id((me + i) % DEV), device_id_type=MESH
        )
        return carry

    lax.fori_loop(1, DEV, greet, 0)

    def load(comp, i):
        rows = pl.ds(pl.multiple_of(8 * i, 8), 8)
        return pltpu.make_async_copy(
            (g1_ref, g2_ref)[comp].at[rows], x_ref.at[comp, rows], in_sem.at[comp, i]
        )

    def start_load(i, carry):
        load(0, i).start()
        load(1, i).start()
        return carry

    lax.fori_loop(0, 16, start_load, 0)

    def rows_step(i, carry):
        load(0, i).wait()
        load(1, i).wait()
        row_butterflies(i, x_ref, tw_ref, yr_ref)
        return carry

    lax.fori_loop(0, 16, rows_step, 0)
    pl.semaphore_wait(barrier, DEV - 1)

    def go(half, dest):
        @pl.when(dest != me)
        def _():
            pltpu.make_async_remote_copy(
                src_ref=send_ref.at[half, dest],
                dst_ref=recv_ref.at[half, me],
                send_sem=go_send.at[half],
                recv_sem=go_recv.at[half],
                device_id=mesh_id(dest),
                device_id_type=MESH,
            ).start()

    def go_own(half):
        return pltpu.make_async_copy(
            send_ref.at[half, me], recv_ref.at[half, me], own_sem.at[half]
        )

    def matmul_step(i, carry):
        k = (me // 8 + i) % 16
        row_matmul(k, wr_ref, yr_ref, send_ref)
        for e in range(8):
            go(0, 8 * k + (me + e) % 8)
        return carry

    lax.fori_loop(0, 16, matmul_step, 0)
    go_own(0).start()
    go_own(1).start()

    def second(i, carry):
        go(1, 8 * ((me // 8 + i // 8) % 16) + (me + i) % 8)
        return carry

    lax.fori_loop(0, DEV, second, 0)

    sub = lax.broadcasted_iota(jnp.int32, (8, L), 0)
    scale = np.float32(1.0 / (N * N))
    w = [[wgt_ref[j, b] * scale for b in range(j + 1)] for j in range(BINS)]

    def all_but_one(src, dst, send, recv, half):
        return pltpu.make_async_remote_copy(
            src_ref=src.at[half, pl.ds(0, DEV - 1)],
            dst_ref=dst.at[half, pl.ds(0, DEV - 1)],
            send_sem=send.at[half],
            recv_sem=recv.at[half],
            device_id=mesh_id(me),
            device_id_type=MESH,
        )

    def ret_own(half):
        return pltpu.make_async_copy(
            ret_ref.at[half, me], out_ref.at[half, me], own_sem.at[2 + half]
        )

    def half_step(half, carry):
        packed = jnp.logical_and(sub == 0, jnp.logical_and(me == 0, half == 0))
        go_own(half).wait()
        all_but_one(send_ref, recv_ref, go_send, go_recv, half).wait_recv()

        def forward(b, c):
            col_forward(half, b, packed, recv_ref, tw_ref, y_ref)
            return c

        def middle(g, c):
            col_middle(half, g, me, packed, w, tw_ref, wf_ref, wi_ref, y_ref, z_ref)
            return c

        def inverse(i, c):
            j = (me // 32 + i) % BINS
            col_inverse(half, j, z_ref, ret_ref)

            def ret(e, c2):
                dest = 32 * j + (me + e) % 32

                @pl.when(dest != me)
                def _():
                    pltpu.make_async_remote_copy(
                        src_ref=ret_ref.at[half, dest],
                        dst_ref=out_ref.at[half, me],
                        send_sem=ret_send.at[half],
                        recv_sem=ret_recv.at[half],
                        device_id=mesh_id(dest),
                        device_id_type=MESH,
                    ).start()

                return c2

            return lax.fori_loop(0, 32, ret, c)

        lax.fori_loop(0, BINS, forward, 0)
        lax.fori_loop(0, A // GROUP, middle, 0)
        lax.fori_loop(0, BINS, inverse, 0)
        ret_own(half).start()
        return carry

    lax.fori_loop(0, 2, half_step, 0)

    def finish(half, carry):
        all_but_one(send_ref, recv_ref, go_send, go_recv, half).wait_send()
        all_but_one(ret_ref, out_ref, ret_send, ret_recv, half).wait_send()
        all_but_one(ret_ref, out_ref, ret_send, ret_recv, half).wait_recv()
        ret_own(half).wait()
        return carry

    lax.fori_loop(0, 2, finish, 0)


def main_stage(g1, g2, weights, tab):
    vmem = pl.BlockSpec(memory_space=pltpu.VMEM)
    hbm = pl.BlockSpec(memory_space=pl.ANY)
    return pl.pallas_call(
        main_kernel,
        in_specs=[pl.BlockSpec(memory_space=pltpu.SMEM), hbm, hbm, vmem, vmem, vmem, vmem],
        out_specs=hbm,
        out_shape=jax.ShapeDtypeStruct((2, DEV, 2, 8, L), F32),
        scratch_shapes=[
            pltpu.VMEM((2, 128, N), F32),
            pltpu.VMEM((16, 256, 256), F32),
            pltpu.VMEM((2, DEV, 2, 8, 256), F32),
            pltpu.VMEM((2, DEV, 2, 8, 256), F32),
            pltpu.VMEM((A, 64, 256), F32),
            pltpu.VMEM((A, 32, 256), F32),
            pltpu.VMEM((2, DEV, 2, 8, L), F32),
            pltpu.SemaphoreType.DMA((2, 16)),
            pltpu.SemaphoreType.DMA((2,)),
            pltpu.SemaphoreType.DMA((2,)),
            pltpu.SemaphoreType.DMA((2,)),
            pltpu.SemaphoreType.DMA((2,)),
            pltpu.SemaphoreType.DMA((4,)),
        ],
        compiler_params=pltpu.CompilerParams(
            collective_id=0, has_side_effects=True, vmem_limit_bytes=62 * 2**20
        ),
        name="main",
    )(weights, g1.reshape(128, N), g2.reshape(128, N), tab["twid"], tab["row"], tab["colf"], tab["coli"])


def back_kernel(x_ref, tw_ref, w_ref, out_ref, z_ref):
    i = pl.program_id(0)

    @pl.when(i < 16)
    def _():
        parts = [x_ref[h, d, c] for c in range(2) for h in range(2) for d in range(8)]
        hi, lo = split(jnp.concatenate(parts, axis=0).T)
        sel = jnp.minimum(i, 1)
        dot = functools.partial(jnp.dot, preferred_element_type=F32)
        Z = dot(hi, w_ref[sel, 0]) + (dot(lo, w_ref[sel, 0]) + dot(hi, w_ref[sel, 1]))
        c, s = tw_ref[i, 0, 0:1], tw_ref[i, 1, 0:1]
        r, m = Z[:, 0:L], Z[:, L : 2 * L]
        z_ref[i, :, 0:L] = r * c - m * s
        z_ref[i, :, L : 2 * L] = m * c + r * s

    @pl.when(i >= 16)
    def _():
        for j in range(ROWS // 8):
            rows = pl.ds(pl.multiple_of((i - 16) * ROWS + 8 * j, 8), 8)
            X = [(z_ref[0, rows, 0:L], None)]
            X += [(z_ref[k, rows, 0:L], z_ref[k, rows, L : 2 * L]) for k in range(1, 16)]
            X += [(z_ref[0, rows, L : 2 * L], None)]
            for p, v in enumerate(irfft(X, A)):
                out_ref[8 * j : 8 * j + 8, L * p : L * p + L] = v


def back_stage(x, tab):
    return pl.pallas_call(
        back_kernel,
        grid=(16 + STEPS,),
        in_specs=[
            pl.BlockSpec((2, 8, 2, 8, L), lambda i: (0, jnp.minimum(i, 15), 0, 0, 0)),
            pl.BlockSpec((A, 2, 8, L), lambda i: (0, 0, 0, 0)),
            pl.BlockSpec((2, 2, 256, 256), lambda i: (0, 0, 0, 0)),
        ],
        out_specs=pl.BlockSpec((ROWS, N), lambda i: (jnp.maximum(i - 16, 0), 0)),
        out_shape=jax.ShapeDtypeStruct((128, N), F32),
        scratch_shapes=[pltpu.VMEM((16, 128, 256), F32)],
        name="back",
    )(x, tab["twid"], tab["back"])


def on_device(shear_one, shear_two, weights):
    tab = {k: jnp.asarray(v) for k, v in tables().items()}
    x = main_stage(shear_one, shear_two, weights, tab)
    return back_stage(x, tab).reshape(1, 128, N)


def solution(mesh):
    spec = P("bin", "tile", None)
    return jax.shard_map(
        on_device, mesh=mesh, in_specs=(spec, spec, P()), out_specs=spec, check_vma=False
    )
```

```python
import functools

import jax
import jax.numpy as jnp
import ml_dtypes
import numpy as np
from jax import lax
from jax.experimental import pallas as pl
from jax.experimental.pallas import tpu as pltpu
from jax.sharding import PartitionSpec as P

N = 4096
A = 32
L = 128
DEV = 128
BINS = 4
F32 = jnp.float32
BF16 = jnp.bfloat16


def hi_lo(matrix):
    hi = matrix.astype(ml_dtypes.bfloat16)
    lo = (matrix - hi.astype(np.float64)).astype(ml_dtypes.bfloat16)
    return np.stack([hi, lo])


def tables():
    lane = np.arange(L)
    angle = 2.0 * np.pi * ((lane[:, None] * lane[None, :]) % L) / L
    c, s = np.cos(angle), np.sin(angle)
    fwd = np.block([[c, s], [-s, c]])
    slot = np.arange(64)
    a0 = 2.0 * np.pi * ((slot[:, None] * lane[None, :]) % L) / L
    a16 = 2.0 * np.pi * (((16 + 32 * slot[:, None]) * lane[None, :]) % N) / N
    first = np.zeros((256, 256))
    first[0:64, 0:128] = np.cos(a0)
    first[128:192, 0:128] = -np.sin(a0)
    first[128, 0:128] = (-1.0) ** lane
    first[64:128, 128:256] = np.cos(a16)
    first[192:256, 128:256] = -np.sin(a16)
    last = 2.0 * first.copy()
    last[0, 0:128] = 1.0
    last[128, 0:128] = (-1.0) ** lane
    k = np.arange(A)
    tw = 2.0 * np.pi * ((k[:, None] * lane[None, :]) % N) / N
    twid = np.stack([np.cos(tw), np.sin(tw)], 1).astype(np.float32)
    twid = np.broadcast_to(twid[:, :, None, :], (A, 2, 8, L)).copy()
    return dict(
        row=np.stack([hi_lo(first), hi_lo(fwd)]),
        colf=hi_lo(fwd.T),
        coli=hi_lo(fwd),
        back=np.stack([hi_lo(last), hi_lo(fwd)]),
        twid=twid,
    )


def fft(xs, sign):
    n = len(xs)
    if n == 1:
        return xs
    even, odd = fft(xs[0::2], sign), fft(xs[1::2], sign)
    out = [None] * n
    h = n // 2
    root = np.float32(np.sqrt(0.5))
    for k in range(h):
        er, ei = even[k]
        r, i = odd[k]
        if k == 0:
            tr, ti = r, i
        elif 4 * k == n:
            tr, ti = (-i, r) if sign > 0 else (i, -r)
            if sign > 0:
                out[k], out[k + h] = (er - i, ei + r), (er + i, ei - r)
            else:
                out[k], out[k + h] = (er + i, ei - r), (er - i, ei + r)
            continue
        elif 8 * k == n:
            tr, ti = ((r - i) * root, (r + i) * root) if sign > 0 else ((r + i) * root, (i - r) * root)
        elif 8 * k == 3 * n:
            if sign > 0:
                pr, pi = (r + i) * root, (r - i) * root
                out[k], out[k + h] = (er - pr, ei + pi), (er + pr, ei - pi)
            else:
                pr, pi = (i - r) * root, (r + i) * root
                out[k], out[k + h] = (er + pr, ei - pi), (er - pr, ei + pi)
            continue
        else:
            c = np.float32(np.cos(2 * np.pi * k / n))
            s = np.float32(sign * np.sin(2 * np.pi * k / n))
            tr, ti = r * c - i * s, r * s + i * c
        out[k], out[k + h] = (er + tr, ei + ti), (er - tr, ei - ti)
    return out


def rfft(xs):
    n = len(xs)
    if n == 2:
        return [(xs[0] + xs[1], None), (xs[0] - xs[1], None)]
    even, odd = rfft(xs[0::2]), rfft(xs[1::2])
    out = [None] * (n // 2 + 1)
    for k in range(n // 4 + 1):
        if k == 0:
            out[0] = (even[0][0] + odd[0][0], None)
            out[n // 2] = (even[0][0] - odd[0][0], None)
        elif 4 * k == n:
            out[k] = (even[k][0], -odd[k][0])
        else:
            er, ei = even[k]
            r, i = odd[k]
            if 8 * k == n:
                root = np.float32(np.sqrt(0.5))
                tr, ti = (r + i) * root, (i - r) * root
            else:
                c = np.float32(np.cos(2 * np.pi * k / n))
                s = np.float32(np.sin(2 * np.pi * k / n))
                tr, ti = r * c + i * s, i * c - r * s
            out[k] = (er + tr, ei + ti)
            out[n // 2 - k] = (er - tr, ti - ei)
    return out


def irfft(X, n):
    if n == 2:
        a, b = X[0][0], X[1][0]
        return [a + b, a - b]
    h = n // 2
    even, odd = [None] * (h // 2 + 1), [None] * (h // 2 + 1)
    for k in range(h // 2 + 1):
        if k == 0:
            even[0] = (X[0][0] + X[h][0], None)
            odd[0] = (X[0][0] - X[h][0], None)
        elif 2 * k == h:
            even[k] = (X[k][0] + X[k][0], None)
            odd[k] = (-(X[k][1] + X[k][1]), None)
        else:
            ar, ai = X[k]
            br, bi = X[h - k]
            even[k] = (ar + br, ai - bi)
            dr, di = ar - br, ai + bi
            if 4 * k == h:
                root = np.float32(np.sqrt(0.5))
                odd[k] = ((dr - di) * root, (dr + di) * root)
            else:
                c = np.float32(np.cos(2 * np.pi * k / n))
                s = np.float32(np.sin(2 * np.pi * k / n))
                odd[k] = (dr * c - di * s, dr * s + di * c)
    e, o = irfft(even, h), irfft(odd, h)
    out = [None] * n
    out[0::2] = e
    out[1::2] = o
    return out


def split(x):
    hi = x.astype(BF16)
    lo = (x - hi.astype(F32)).astype(BF16)
    return hi, lo


ROWS = 16
STEPS = 128 // ROWS
GROUP = 4
FLAT = pl.DeviceIdType.LOGICAL


def row_butterflies(comp, i, x_ref, tw_ref, y_ref):
    rows = pl.ds(pl.multiple_of(8 * i, 8), 8)
    X = rfft([x_ref[comp, rows, L * p : L * p + L] for p in range(A)])
    y_ref[0, rows, 0:L] = X[0][0]
    y_ref[0, rows, L : 2 * L] = X[16][0]
    for k in range(1, 16):
        r, m = X[k]
        c, s = tw_ref[k, 0], tw_ref[k, 1]
        y_ref[k, rows, 0:L] = r * c + m * s
        y_ref[k, rows, L : 2 * L] = m * c - r * s


def row_matmul(comp, k, w_ref, y_ref, send_ref):
    hi, lo = split(y_ref[k])
    sel = jnp.minimum(k, 1)
    whi, wlo = w_ref[sel, 0], w_ref[sel, 1]
    dims = (((1,), (1,)), ((), ()))
    dot = functools.partial(lax.dot_general, dimension_numbers=dims, preferred_element_type=F32)
    out = dot(whi, hi) + (dot(whi, lo) + dot(wlo, hi))
    for h in range(2):
        for c in range(2):
            for d in range(8):
                at = 128 * c + 64 * h + 8 * d
                send_ref[h, 8 * k + d, comp, c] = out[at : at + 8]


def col_forward(half, b, packed, x_ref, tw_ref, y_ref):
    lane = lax.broadcasted_iota(jnp.int32, (8, L), 1)
    sign = jnp.where(lane % 2 == 0, 1.0, -1.0).astype(F32)
    total = x_ref[half, A * b, 1, 1]
    for t in range(1, A):
        total = total + x_ref[half, A * b + t, 1, 1]
    corner = sign * (jnp.sum(total * sign, axis=1, keepdims=True) * np.float32(-1.0 / N))
    for R in range(2):
        xs = []
        for t in range(A):
            re = x_ref[half, A * b + t, R, 0]
            im = x_ref[half, A * b + t, R, 1]
            if R == 0:
                im = jnp.where(packed, corner, im)
            else:
                re = jnp.where(packed, 0.0, re)
                im = jnp.where(packed, x_ref[half, A * b + t, 0, 1], im)
            xs.append((re, im))
        X = fft(xs, -1)
        rows = pl.ds(pl.multiple_of(32 * R + 8 * b, 8), 8)
        for k in range(A):
            r, m = X[k]
            if k:
                c, s = tw_ref[k, 0], tw_ref[k, 1]
                r, m = r * c + m * s, m * c - r * s
            y_ref[k, rows, 0:L] = r
            y_ref[k, rows, L : 2 * L] = m


def col_middle(half, g, me, packed, w, tw_ref, wf_ref, wi_ref, y_ref, z_ref):
    base = g * GROUP
    group, part = me // 8, me % 8
    sub = lax.broadcasted_iota(jnp.int32, (8, L), 0)
    lane = lax.broadcasted_iota(jnp.int32, (8, L), 1)
    hi, lo = split(y_ref[pl.ds(base, GROUP)].reshape(GROUP * 64, 256))
    dot = functools.partial(jnp.dot, preferred_element_type=F32)
    G = dot(hi, wf_ref[0]) + (dot(lo, wf_ref[0]) + dot(hi, wf_ref[1]))
    at = 8 * part + sub
    col = jnp.where(group == 0, 32 * at + 16 * half, group + 32 * (64 * half + at))
    col = jnp.where(col < N // 2, col, col - N).astype(F32)
    rows = []
    for kk in range(GROUP):
        u = base + kk + A * lane
        nyquist = u == N // 2
        row = jnp.where(u < N // 2, u, u - N).astype(F32)
        row2 = row * row

        def kern(l1):
            q = jnp.maximum(l1 * l1 + row2, 1.0)
            return (l1 * l1 - row2) / q, (2.0 * l1) * row / q

        a, b = kern(col)
        ar, ai = a, jnp.where(nyquist, -b, 0.0)
        a2, b2 = kern(np.float32(-N // 2))
        br = jnp.where(packed, a2, jnp.where(nyquist, 0.0, b))
        bi = jnp.where(jnp.logical_and(packed, jnp.logical_not(nyquist)), -b2, 0.0)
        H = []
        for b_ in range(BINS):
            o1, o2 = kk * 64 + 8 * b_, kk * 64 + 32 + 8 * b_
            g1r, g1i = G[o1 : o1 + 8, 0:L], G[o1 : o1 + 8, L : 2 * L]
            g2r, g2i = G[o2 : o2 + 8, 0:L], G[o2 : o2 + 8, L : 2 * L]
            hr = ar * g1r - ai * g1i + br * g2r - bi * g2i
            hm = ar * g1i + ai * g1r + br * g2i + bi * g2r
            H.append((hr, hm))
        for j in range(BINS):
            fr, fi = H[0][0] * w[j][0], H[0][1] * w[j][0]
            for b_ in range(1, j + 1):
                fr, fi = fr + H[b_][0] * w[j][b_], fi + H[b_][1] * w[j][b_]
            rows.append(jnp.concatenate([fr, fi], axis=1))
    hi, lo = split(jnp.concatenate(rows, axis=0))
    Z = dot(hi, wi_ref[0]) + (dot(lo, wi_ref[0]) + dot(hi, wi_ref[1]))
    for kk in range(GROUP):
        c, s = tw_ref[base + kk, 0], tw_ref[base + kk, 1]
        for j in range(BINS):
            o = 32 * kk + 8 * j
            r, m = Z[o : o + 8, 0:L], Z[o : o + 8, L : 2 * L]
            z_ref[base + kk, 8 * j : 8 * j + 8, 0:L] = r * c - m * s
            z_ref[base + kk, 8 * j : 8 * j + 8, L : 2 * L] = m * c + r * s


def col_inverse(half, j, z_ref, ret_ref):
    rows = pl.ds(pl.multiple_of(8 * j, 8), 8)
    xs = [(z_ref[k, rows, 0:L], z_ref[k, rows, L : 2 * L]) for k in range(A)]
    for t, (r, m) in enumerate(fft(xs, 1)):
        ret_ref[half, A * j + t, 0] = r
        ret_ref[half, A * j + t, 1] = m


def back_matmul(k, in_ref, tw_ref, w_ref, z_ref):
    parts = [in_ref[h, 8 * k + d, c] for c in range(2) for h in range(2) for d in range(8)]
    hi, lo = split(jnp.concatenate(parts, axis=0).T)
    sel = jnp.minimum(k, 1)
    dot = functools.partial(jnp.dot, preferred_element_type=F32)
    Z = dot(hi, w_ref[sel, 0]) + (dot(lo, w_ref[sel, 0]) + dot(hi, w_ref[sel, 1]))
    c, s = tw_ref[k, 0, 0:1], tw_ref[k, 1, 0:1]
    r, m = Z[:, 0:L], Z[:, L : 2 * L]
    z_ref[k, :, 0:L] = r * c - m * s
    z_ref[k, :, L : 2 * L] = m * c + r * s


def main_kernel(
    wgt_ref, g1_ref, g2_ref, tw_any, wr_any, wf_any, wi_any, wb_any, out_ref,
    tw_ref, wr_ref, wf_ref, wi_ref, wb_ref,
    x_ref, yr_ref, send_ref, recv_ref, y_ref, z_ref, ret_ref, land_ref, last_ref,
    tab_sem, in_sem, go_send, go_recv, ret_send, ret_recv, out_sem,
):
    mybin, mytile = lax.axis_index("bin"), lax.axis_index("tile")
    me = mybin * 32 + mytile
    mygroup, mypart = mybin * 4 + lax.div(mytile, 8), lax.rem(mytile, 8)

    barrier = pltpu.get_barrier_semaphore()

    def greet(i, carry):
        pl.semaphore_signal(
            barrier, inc=1, device_id=lax.rem(me + i, DEV), device_id_type=FLAT
        )
        return carry

    tabs = [
        pltpu.make_async_copy(a, b, tab_sem.at[i])
        for i, (a, b) in enumerate(
            zip((tw_any, wr_any, wf_any, wi_any, wb_any), (tw_ref, wr_ref, wf_ref, wi_ref, wb_ref))
        )
    ]

    def load(comp, i):
        rows = pl.ds(pl.multiple_of(32 * i, 32), 32)
        return pltpu.make_async_copy(
            (g1_ref, g2_ref)[comp].at[rows], x_ref.at[comp, rows], in_sem.at[comp, i]
        )

    tabs[0].start()
    for i in range(4):
        load(0, i).start()
    tabs[1].start()
    for i in range(4):
        load(1, i).start()
    for t in tabs[2:]:
        t.start()
    lax.fori_loop(1, DEV, greet, 0)
    tabs[0].wait()

    def go(half, dest, comp):
        at = (half, dest) if comp is None else (half, dest, comp)
        to = (half, me) if comp is None else (half, me, comp)
        pltpu.make_async_remote_copy(
            src_ref=send_ref.at[at],
            dst_ref=recv_ref.at[to],
            send_sem=go_send.at[half],
            recv_sem=go_recv.at[half],
            device_id=dest,
            device_id_type=FLAT,
        ).start()

    def rows_of(comp):
        def some_rows(i, carry):
            load(comp, i).wait()

            def step(j, c):
                row_butterflies(comp, 4 * i + j, x_ref, tw_ref, yr_ref)
                return c

            return lax.fori_loop(0, 4, step, carry)

        def matmul_step(i, carry):
            k = lax.rem(mygroup + i, 16)
            row_matmul(comp, k, wr_ref, yr_ref, send_ref)

            @pl.when(i > 0)
            def _():
                go(0, 8 * k + mypart, comp)

            for e in range(1, 8):
                go(0, 8 * k + lax.rem(mypart + e, 8), comp)
            return carry

        lax.fori_loop(0, 4, some_rows, 0)
        if comp == 0:
            tabs[1].wait()
            pl.semaphore_wait(barrier, DEV - 1)
        lax.fori_loop(0, 16, matmul_step, 0)

    rows_of(0)
    rows_of(1)
    for half in range(2):
        pltpu.make_async_copy(
            send_ref.at[half, me], recv_ref.at[half, me], go_recv.at[half]
        ).start()

    def second(i, carry):
        go(1, 8 * lax.rem(mygroup + lax.div(i, 8), 16) + lax.rem(mypart + i, 8), None)
        return carry

    lax.fori_loop(1, DEV, second, 0)
    for t in tabs[2:]:
        t.wait()

    sub = lax.broadcasted_iota(jnp.int32, (8, L), 0)
    scale = np.float32(1.0 / (N * N))
    w = [[wgt_ref[j, b] * scale for b in range(j + 1)] for j in range(BINS)]

    def half_step(half, carry):
        packed = jnp.logical_and(sub == 0, jnp.logical_and(me == 0, half == 0))
        pltpu.make_async_copy(send_ref.at[half], recv_ref.at[half], go_recv.at[half]).wait()

        def forward(b, c):
            col_forward(half, b, packed, recv_ref, tw_ref, y_ref)
            return c

        def middle(g, c):
            col_middle(half, g, me, packed, w, tw_ref, wf_ref, wi_ref, y_ref, z_ref)
            return c

        def inverse(i, c):
            j = lax.rem(mybin + i, BINS)
            col_inverse(half, j, z_ref, ret_ref)

            def ret(dest):
                pltpu.make_async_remote_copy(
                    src_ref=ret_ref.at[half, dest],
                    dst_ref=land_ref.at[half, me],
                    send_sem=ret_send.at[half],
                    recv_sem=ret_recv.at[half, mygroup],
                    device_id=dest,
                    device_id_type=FLAT,
                ).start()

            def ret_step(e, c2):
                z = lax.rem(lax.div(mytile, 8) + lax.div(e, 8), 4)
                ret(32 * j + 8 * z + lax.rem(mypart + e, 8))
                return c2

            @pl.when(i > 0)
            def _():
                ret(32 * j + mytile)

            return lax.fori_loop(1, 32, ret_step, c)

        lax.fori_loop(0, BINS, forward, 0)
        lax.fori_loop(0, A // GROUP, middle, 0)
        lax.fori_loop(0, BINS, inverse, 0)
        pltpu.make_async_copy(
            ret_ref.at[half, me], land_ref.at[half, me], ret_recv.at[half, mygroup]
        ).start()
        return carry

    lax.fori_loop(0, 2, half_step, 0)

    def write(k):
        return pltpu.make_async_copy(last_ref.at[k], out_ref.at[k], out_sem.at[k])

    def back_step(i, carry):
        b = lax.rem(mybin + 4 - lax.div(i, 4), 4)
        z = lax.rem(lax.div(mytile, 8) + 4 - lax.rem(i, 4), 4)
        k = 4 * b + z
        eight = pl.ds(pl.multiple_of(8 * k, 8), 8)
        for half in range(2):
            pltpu.make_async_copy(
                ret_ref.at[half, eight], land_ref.at[half, eight], ret_recv.at[half, k]
            ).wait()
        back_matmul(k, land_ref, tw_ref, wb_ref, last_ref)
        write(k).start()
        return carry

    lax.fori_loop(0, 16, back_step, 0)

    def finish(half, carry):
        for src, sem in ((send_ref, go_send), (ret_ref, ret_send)):
            part = src.at[half, pl.ds(0, DEV - 1)]
            pltpu.make_async_remote_copy(
                src_ref=part, dst_ref=part, send_sem=sem.at[half], recv_sem=sem.at[half],
                device_id=me, device_id_type=FLAT,
            ).wait_send()
        return carry

    lax.fori_loop(0, 2, finish, 0)

    def written(k, carry):
        write(k).wait()
        return carry

    lax.fori_loop(0, 16, written, 0)


def main_stage(g1, g2, weights, tab):
    hbm = pl.BlockSpec(memory_space=pl.ANY)
    return pl.pallas_call(
        main_kernel,
        in_specs=[pl.BlockSpec(memory_space=pltpu.SMEM)] + [hbm] * 7,
        out_specs=hbm,
        out_shape=jax.ShapeDtypeStruct((16, 128, 256), F32),
        scratch_shapes=[
            pltpu.VMEM((A, 2, 8, L), F32),
            pltpu.VMEM((2, 2, 256, 256), BF16),
            pltpu.VMEM((2, 256, 256), BF16),
            pltpu.VMEM((2, 256, 256), BF16),
            pltpu.VMEM((2, 2, 256, 256), BF16),
            pltpu.VMEM((2, 128, N), F32),
            pltpu.VMEM((16, 128, 256), F32),
            pltpu.VMEM((2, DEV, 2, 2, 8, L), F32),
            pltpu.VMEM((2, DEV, 2, 2, 8, L), F32),
            pltpu.VMEM((A, 64, 256), F32),
            pltpu.VMEM((A, 32, 256), F32),
            pltpu.VMEM((2, DEV, 2, 8, L), F32),
            pltpu.VMEM((2, DEV, 2, 8, L), F32),
            pltpu.VMEM((16, 128, 256), F32),
            pltpu.SemaphoreType.DMA((5,)),
            pltpu.SemaphoreType.DMA((2, 4)),
            pltpu.SemaphoreType.DMA((2,)),
            pltpu.SemaphoreType.DMA((2,)),
            pltpu.SemaphoreType.DMA((2,)),
            pltpu.SemaphoreType.DMA((2, 16)),
            pltpu.SemaphoreType.DMA((16,)),
        ],
        compiler_params=pltpu.CompilerParams(
            collective_id=0, has_side_effects=True, vmem_limit_bytes=62 * 2**20
        ),
        name="main",
    )(
        weights, g1.reshape(128, N), g2.reshape(128, N),
        tab["twid"], tab["row"], tab["colf"], tab["coli"], tab["back"],
    )


def last_kernel(z_ref, out_ref):
    for j in range(ROWS // 8):
        rows = slice(8 * j, 8 * j + 8)
        X = [(z_ref[0, rows, 0:L], None)]
        X += [(z_ref[k, rows, 0:L], z_ref[k, rows, L : 2 * L]) for k in range(1, 16)]
        X += [(z_ref[0, rows, L : 2 * L], None)]
        for p, v in enumerate(irfft(X, A)):
            out_ref[rows, L * p : L * p + L] = v


def last_stage(z):
    return pl.pallas_call(
        last_kernel,
        grid=(STEPS,),
        in_specs=[pl.BlockSpec((16, ROWS, 256), lambda i: (0, i, 0))],
        out_specs=pl.BlockSpec((ROWS, N), lambda i: (i, 0)),
        out_shape=jax.ShapeDtypeStruct((128, N), F32),
        name="last",
    )(z)


def on_device(shear_one, shear_two, weights):
    tab = {k: jnp.asarray(v) for k, v in tables().items()}
    z = main_stage(shear_one, shear_two, weights, tab)
    return last_stage(z).reshape(1, 128, N)


def solution(mesh):
    spec = P("bin", "tile", None)
    return jax.shard_map(
        on_device, mesh=mesh, in_specs=(spec, spec, P()), out_specs=spec, check_vma=False
    )
```

```python
import functools

import jax
import jax.numpy as jnp
import ml_dtypes
import numpy as np
from jax import lax
from jax.experimental import pallas as pl
from jax.experimental.pallas import tpu as pltpu
from jax.sharding import PartitionSpec as P

N = 4096
A = 32
L = 128
DEV = 128
BINS = 4
F32 = jnp.float32
BF16 = jnp.bfloat16


def hi_lo(matrix):
    hi = matrix.astype(ml_dtypes.bfloat16)
    lo = (matrix - hi.astype(np.float64)).astype(ml_dtypes.bfloat16)
    return np.stack([hi, lo])


def tables():
    lane = np.arange(L)
    angle = 2.0 * np.pi * ((lane[:, None] * lane[None, :]) % L) / L
    c, s = np.cos(angle), np.sin(angle)
    fwd = np.block([[c, s], [-s, c]])
    slot = np.arange(64)
    a0 = 2.0 * np.pi * ((slot[:, None] * lane[None, :]) % L) / L
    a16 = 2.0 * np.pi * (((16 + 32 * slot[:, None]) * lane[None, :]) % N) / N
    first = np.zeros((256, 256))
    first[0:64, 0:128] = np.cos(a0)
    first[128:192, 0:128] = -np.sin(a0)
    first[128, 0:128] = (-1.0) ** lane
    first[64:128, 128:256] = np.cos(a16)
    first[192:256, 128:256] = -np.sin(a16)
    last = 2.0 * first.copy()
    last[0, 0:128] = 1.0
    last[128, 0:128] = (-1.0) ** lane
    k = np.arange(A)
    tw = 2.0 * np.pi * ((k[:, None] * lane[None, :]) % N) / N
    twid = np.stack([np.cos(tw), np.sin(tw)], 1).astype(np.float32)
    twid = np.broadcast_to(twid[:, :, None, :], (A, 2, 8, L)).copy()
    return dict(
        row=np.stack([hi_lo(first), hi_lo(fwd)]),
        colf=hi_lo(fwd.T),
        coli=hi_lo(fwd),
        back=np.stack([hi_lo(last), hi_lo(fwd)]),
        twid=twid,
    )


def fft(xs, sign):
    n = len(xs)
    if n == 1:
        return xs
    even, odd = fft(xs[0::2], sign), fft(xs[1::2], sign)
    out = [None] * n
    h = n // 2
    root = np.float32(np.sqrt(0.5))
    for k in range(h):
        er, ei = even[k]
        r, i = odd[k]
        if k == 0:
            tr, ti = r, i
        elif 4 * k == n:
            tr, ti = (-i, r) if sign > 0 else (i, -r)
            if sign > 0:
                out[k], out[k + h] = (er - i, ei + r), (er + i, ei - r)
            else:
                out[k], out[k + h] = (er + i, ei - r), (er - i, ei + r)
            continue
        elif 8 * k == n:
            tr, ti = ((r - i) * root, (r + i) * root) if sign > 0 else ((r + i) * root, (i - r) * root)
        elif 8 * k == 3 * n:
            if sign > 0:
                pr, pi = (r + i) * root, (r - i) * root
                out[k], out[k + h] = (er - pr, ei + pi), (er + pr, ei - pi)
            else:
                pr, pi = (i - r) * root, (r + i) * root
                out[k], out[k + h] = (er + pr, ei - pi), (er - pr, ei + pi)
            continue
        else:
            c = np.float32(np.cos(2 * np.pi * k / n))
            s = np.float32(sign * np.sin(2 * np.pi * k / n))
            tr, ti = r * c - i * s, r * s + i * c
        out[k], out[k + h] = (er + tr, ei + ti), (er - tr, ei - ti)
    return out


def rfft(xs):
    n = len(xs)
    if n == 2:
        return [(xs[0] + xs[1], None), (xs[0] - xs[1], None)]
    even, odd = rfft(xs[0::2]), rfft(xs[1::2])
    out = [None] * (n // 2 + 1)
    for k in range(n // 4 + 1):
        if k == 0:
            out[0] = (even[0][0] + odd[0][0], None)
            out[n // 2] = (even[0][0] - odd[0][0], None)
        elif 4 * k == n:
            out[k] = (even[k][0], -odd[k][0])
        else:
            er, ei = even[k]
            r, i = odd[k]
            if 8 * k == n:
                root = np.float32(np.sqrt(0.5))
                tr, ti = (r + i) * root, (i - r) * root
            else:
                c = np.float32(np.cos(2 * np.pi * k / n))
                s = np.float32(np.sin(2 * np.pi * k / n))
                tr, ti = r * c + i * s, i * c - r * s
            out[k] = (er + tr, ei + ti)
            out[n // 2 - k] = (er - tr, ti - ei)
    return out


def irfft(X, n):
    if n == 2:
        a, b = X[0][0], X[1][0]
        return [a + b, a - b]
    h = n // 2
    even, odd = [None] * (h // 2 + 1), [None] * (h // 2 + 1)
    for k in range(h // 2 + 1):
        if k == 0:
            even[0] = (X[0][0] + X[h][0], None)
            odd[0] = (X[0][0] - X[h][0], None)
        elif 2 * k == h:
            even[k] = (X[k][0] + X[k][0], None)
            odd[k] = (-(X[k][1] + X[k][1]), None)
        else:
            ar, ai = X[k]
            br, bi = X[h - k]
            even[k] = (ar + br, ai - bi)
            dr, di = ar - br, ai + bi
            if 4 * k == h:
                root = np.float32(np.sqrt(0.5))
                odd[k] = ((dr - di) * root, (dr + di) * root)
            else:
                c = np.float32(np.cos(2 * np.pi * k / n))
                s = np.float32(np.sin(2 * np.pi * k / n))
                odd[k] = (dr * c - di * s, dr * s + di * c)
    e, o = irfft(even, h), irfft(odd, h)
    out = [None] * n
    out[0::2] = e
    out[1::2] = o
    return out


def split(x):
    hi = x.astype(BF16)
    lo = (x - hi.astype(F32)).astype(BF16)
    return hi, lo


ROWS = 64
STEPS = 128 // ROWS
GROUP = 4
FLAT = pl.DeviceIdType.LOGICAL


def row_butterflies(comp, i, x_ref, tw_ref, y_ref):
    rows = pl.ds(pl.multiple_of(8 * i, 8), 8)
    X = rfft([x_ref[comp, rows, L * p : L * p + L] for p in range(A)])
    y_ref[0, rows, 0:L] = X[0][0]
    y_ref[0, rows, L : 2 * L] = X[16][0]
    for k in range(1, 16):
        r, m = X[k]
        c, s = tw_ref[k, 0], tw_ref[k, 1]
        y_ref[k, rows, 0:L] = r * c + m * s
        y_ref[k, rows, L : 2 * L] = m * c - r * s


def row_matmul(comp, k, w_ref, y_ref, send_ref):
    hi, lo = split(y_ref[k])
    sel = jnp.minimum(k, 1)
    whi, wlo = w_ref[sel, 0], w_ref[sel, 1]
    dims = (((1,), (1,)), ((), ()))
    dot = functools.partial(lax.dot_general, dimension_numbers=dims, preferred_element_type=F32)
    out = dot(whi, hi) + (dot(whi, lo) + dot(wlo, hi))
    for h in range(2):
        for c in range(2):
            for d in range(8):
                at = 128 * c + 64 * h + 8 * d
                send_ref[h, 8 * k + d, comp, c] = out[at : at + 8]


def col_forward(half, b, packed, x_ref, tw_ref, y_ref):
    lane = lax.broadcasted_iota(jnp.int32, (8, L), 1)
    sign = jnp.where(lane % 2 == 0, 1.0, -1.0).astype(F32)
    total = x_ref[half, A * b, 1, 1]
    for t in range(1, A):
        total = total + x_ref[half, A * b + t, 1, 1]
    corner = sign * (jnp.sum(total * sign, axis=1, keepdims=True) * np.float32(-1.0 / N))
    for R in range(2):
        xs = []
        for t in range(A):
            re = x_ref[half, A * b + t, R, 0]
            im = x_ref[half, A * b + t, R, 1]
            if R == 0:
                im = jnp.where(packed, corner, im)
            else:
                re = jnp.where(packed, 0.0, re)
                im = jnp.where(packed, x_ref[half, A * b + t, 0, 1], im)
            xs.append((re, im))
        X = fft(xs, -1)
        rows = pl.ds(pl.multiple_of(32 * R + 8 * b, 8), 8)
        for k in range(A):
            r, m = X[k]
            if k:
                c, s = tw_ref[k, 0], tw_ref[k, 1]
                r, m = r * c + m * s, m * c - r * s
            y_ref[k, rows, 0:L] = r
            y_ref[k, rows, L : 2 * L] = m


def col_middle(half, g, me, packed, w, tw_ref, wf_ref, wi_ref, y_ref, z_ref):
    base = g * GROUP
    group, part = me // 8, me % 8
    sub = lax.broadcasted_iota(jnp.int32, (8, L), 0)
    lane = lax.broadcasted_iota(jnp.int32, (8, L), 1)
    hi, lo = split(y_ref[pl.ds(base, GROUP)].reshape(GROUP * 64, 256))
    dot = functools.partial(jnp.dot, preferred_element_type=F32)
    G = dot(hi, wf_ref[0]) + (dot(lo, wf_ref[0]) + dot(hi, wf_ref[1]))
    at = 8 * part + sub
    col = jnp.where(group == 0, 32 * at + 16 * half, group + 32 * (64 * half + at))
    col = jnp.where(col < N // 2, col, col - N).astype(F32)
    rows = []
    for kk in range(GROUP):
        u = base + kk + A * lane
        nyquist = u == N // 2
        row = jnp.where(u < N // 2, u, u - N).astype(F32)
        row2 = row * row

        def kern(l1):
            q = jnp.maximum(l1 * l1 + row2, 1.0)
            return (l1 * l1 - row2) / q, (2.0 * l1) * row / q

        a, b = kern(col)
        ar, ai = a, jnp.where(nyquist, -b, 0.0)
        a2, b2 = kern(np.float32(-N // 2))
        br = jnp.where(packed, a2, jnp.where(nyquist, 0.0, b))
        bi = jnp.where(jnp.logical_and(packed, jnp.logical_not(nyquist)), -b2, 0.0)
        H = []
        for b_ in range(BINS):
            o1, o2 = kk * 64 + 8 * b_, kk * 64 + 32 + 8 * b_
            g1r, g1i = G[o1 : o1 + 8, 0:L], G[o1 : o1 + 8, L : 2 * L]
            g2r, g2i = G[o2 : o2 + 8, 0:L], G[o2 : o2 + 8, L : 2 * L]
            hr = ar * g1r - ai * g1i + br * g2r - bi * g2i
            hm = ar * g1i + ai * g1r + br * g2i + bi * g2r
            H.append((hr, hm))
        for j in range(BINS):
            fr, fi = H[0][0] * w[j][0], H[0][1] * w[j][0]
            for b_ in range(1, j + 1):
                fr, fi = fr + H[b_][0] * w[j][b_], fi + H[b_][1] * w[j][b_]
            rows.append(jnp.concatenate([fr, fi], axis=1))
    hi, lo = split(jnp.concatenate(rows, axis=0))
    Z = dot(hi, wi_ref[0]) + (dot(lo, wi_ref[0]) + dot(hi, wi_ref[1]))
    for kk in range(GROUP):
        c, s = tw_ref[base + kk, 0], tw_ref[base + kk, 1]
        for j in range(BINS):
            o = 32 * kk + 8 * j
            r, m = Z[o : o + 8, 0:L], Z[o : o + 8, L : 2 * L]
            z_ref[base + kk, 8 * j : 8 * j + 8, 0:L] = r * c - m * s
            z_ref[base + kk, 8 * j : 8 * j + 8, L : 2 * L] = m * c + r * s


def col_inverse(half, j, z_ref, ret_ref):
    rows = pl.ds(pl.multiple_of(8 * j, 8), 8)
    xs = [(z_ref[k, rows, 0:L], z_ref[k, rows, L : 2 * L]) for k in range(A)]
    for t, (r, m) in enumerate(fft(xs, 1)):
        ret_ref[half, A * j + t, 0] = r
        ret_ref[half, A * j + t, 1] = m


def back_matmul(k, in_ref, tw_ref, w_ref, z_ref):
    parts = [in_ref[h, 8 * k + d, c] for c in range(2) for h in range(2) for d in range(8)]
    hi, lo = split(jnp.concatenate(parts, axis=0).T)
    sel = jnp.minimum(k, 1)
    dot = functools.partial(jnp.dot, preferred_element_type=F32)
    Z = dot(hi, w_ref[sel, 0]) + (dot(lo, w_ref[sel, 0]) + dot(hi, w_ref[sel, 1]))
    c, s = tw_ref[k, 0, 0:1], tw_ref[k, 1, 0:1]
    r, m = Z[:, 0:L], Z[:, L : 2 * L]
    z_ref[k, :, 0:L] = r * c - m * s
    z_ref[k, :, L : 2 * L] = m * c + r * s


def main_kernel(
    wgt_ref, g1_ref, g2_ref, tw_any, wr_any, wf_any, wi_any, wb_any, out_ref,
    tw_ref, wr_ref, wf_ref, wi_ref, wb_ref,
    x_ref, yr_ref, send_ref, recv_ref, y_ref, z_ref, ret_ref, land_ref, last_ref,
    tab_sem, in_sem, go_send, go_recv, ret_send, ret_recv, out_sem,
):
    mybin, mytile = lax.axis_index("bin"), lax.axis_index("tile")
    me = mybin * 32 + mytile
    mygroup, mypart = mybin * 4 + lax.div(mytile, 8), lax.rem(mytile, 8)

    barrier = pltpu.get_barrier_semaphore()

    def greet(i, carry):
        pl.semaphore_signal(
            barrier, inc=1, device_id=lax.rem(me + i, DEV), device_id_type=FLAT
        )
        return carry

    tabs = [
        pltpu.make_async_copy(a, b, tab_sem.at[i])
        for i, (a, b) in enumerate(
            zip((tw_any, wr_any, wf_any, wi_any, wb_any), (tw_ref, wr_ref, wf_ref, wi_ref, wb_ref))
        )
    ]

    def load(comp, i):
        rows = pl.ds(pl.multiple_of(32 * i, 32), 32)
        return pltpu.make_async_copy(
            (g1_ref, g2_ref)[comp].at[rows], x_ref.at[comp, rows], in_sem.at[comp, i]
        )

    tabs[0].start()
    for i in range(4):
        load(0, i).start()
    tabs[1].start()
    for i in range(4):
        load(1, i).start()
    for t in tabs[2:]:
        t.start()
    lax.fori_loop(1, DEV, greet, 0)
    tabs[0].wait()

    def go(half, dest, comp):
        at = (half, dest) if comp is None else (half, dest, comp)
        to = (half, me) if comp is None else (half, me, comp)
        pltpu.make_async_remote_copy(
            src_ref=send_ref.at[at],
            dst_ref=recv_ref.at[to],
            send_sem=go_send.at[half],
            recv_sem=go_recv.at[half],
            device_id=dest,
            device_id_type=FLAT,
        ).start()

    def rows_of(comp):
        def some_rows(i, carry):
            load(comp, i).wait()

            def step(j, c):
                row_butterflies(comp, 4 * i + j, x_ref, tw_ref, yr_ref)
                return c

            return lax.fori_loop(0, 4, step, carry)

        def matmul_step(i, carry):
            k = lax.rem(mygroup + i, 16)
            row_matmul(comp, k, wr_ref, yr_ref, send_ref)

            @pl.when(i > 0)
            def _():
                go(0, 8 * k + mypart, comp)

            for e in range(1, 8):
                go(0, 8 * k + lax.rem(mypart + e, 8), comp)
            return carry

        lax.fori_loop(0, 4, some_rows, 0)
        if comp == 0:
            tabs[1].wait()
            pl.semaphore_wait(barrier, DEV - 1)
        lax.fori_loop(0, 16, matmul_step, 0)

    rows_of(0)
    rows_of(1)
    for half in range(2):
        pltpu.make_async_copy(
            send_ref.at[half, me], recv_ref.at[half, me], go_recv.at[half]
        ).start()

    def second(i, carry):
        go(1, 8 * lax.rem(mygroup + lax.div(i, 8), 16) + lax.rem(mypart + i, 8), None)
        return carry

    lax.fori_loop(1, DEV, second, 0)
    for t in tabs[2:]:
        t.wait()

    sub = lax.broadcasted_iota(jnp.int32, (8, L), 0)
    scale = np.float32(1.0 / (N * N))
    w = [[wgt_ref[j, b] * scale for b in range(j + 1)] for j in range(BINS)]

    def half_step(half, carry):
        packed = jnp.logical_and(sub == 0, jnp.logical_and(me == 0, half == 0))
        pltpu.make_async_copy(send_ref.at[half], recv_ref.at[half], go_recv.at[half]).wait()

        def forward(b, c):
            col_forward(half, b, packed, recv_ref, tw_ref, y_ref)
            return c

        def middle(g, c):
            col_middle(half, g, me, packed, w, tw_ref, wf_ref, wi_ref, y_ref, z_ref)
            return c

        def inverse(i, c):
            j = lax.rem(mybin + i, BINS)
            col_inverse(half, j, z_ref, ret_ref)

            def ret(dest):
                pltpu.make_async_remote_copy(
                    src_ref=ret_ref.at[half, dest],
                    dst_ref=land_ref.at[half, me],
                    send_sem=ret_send.at[half],
                    recv_sem=ret_recv.at[half, mygroup],
                    device_id=dest,
                    device_id_type=FLAT,
                ).start()

            def ret_step(e, c2):
                z = lax.rem(lax.div(mytile, 8) + lax.div(e, 8), 4)
                ret(32 * j + 8 * z + lax.rem(mypart + e, 8))
                return c2

            @pl.when(i > 0)
            def _():
                ret(32 * j + mytile)

            return lax.fori_loop(1, 32, ret_step, c)

        lax.fori_loop(0, BINS, forward, 0)
        lax.fori_loop(0, A // GROUP, middle, 0)
        lax.fori_loop(0, BINS, inverse, 0)
        pltpu.make_async_copy(
            ret_ref.at[half, me], land_ref.at[half, me], ret_recv.at[half, mygroup]
        ).start()
        return carry

    lax.fori_loop(0, 2, half_step, 0)

    def write(k):
        return pltpu.make_async_copy(last_ref.at[k], out_ref.at[k], out_sem.at[k])

    def back_step(i, carry):
        b = lax.rem(mybin + 4 - lax.div(i, 4), 4)
        z = lax.rem(lax.div(mytile, 8) + 4 - lax.rem(i, 4), 4)
        k = 4 * b + z
        eight = pl.ds(pl.multiple_of(8 * k, 8), 8)
        for half in range(2):
            pltpu.make_async_copy(
                ret_ref.at[half, eight], land_ref.at[half, eight], ret_recv.at[half, k]
            ).wait()
        back_matmul(k, land_ref, tw_ref, wb_ref, last_ref)
        write(k).start()
        return carry

    lax.fori_loop(0, 16, back_step, 0)

    def finish(half, carry):
        for src, sem in ((send_ref, go_send), (ret_ref, ret_send)):
            part = src.at[half, pl.ds(0, DEV - 1)]
            pltpu.make_async_remote_copy(
                src_ref=part, dst_ref=part, send_sem=sem.at[half], recv_sem=sem.at[half],
                device_id=me, device_id_type=FLAT,
            ).wait_send()
        return carry

    lax.fori_loop(0, 2, finish, 0)

    def written(k, carry):
        write(k).wait()
        return carry

    lax.fori_loop(0, 16, written, 0)


def main_stage(g1, g2, weights, tab):
    hbm = pl.BlockSpec(memory_space=pl.ANY)
    return pl.pallas_call(
        main_kernel,
        in_specs=[pl.BlockSpec(memory_space=pltpu.SMEM)] + [hbm] * 7,
        out_specs=hbm,
        out_shape=jax.ShapeDtypeStruct((16, 128, 256), F32),
        scratch_shapes=[
            pltpu.VMEM((A, 2, 8, L), F32),
            pltpu.VMEM((2, 2, 256, 256), BF16),
            pltpu.VMEM((2, 256, 256), BF16),
            pltpu.VMEM((2, 256, 256), BF16),
            pltpu.VMEM((2, 2, 256, 256), BF16),
            pltpu.VMEM((2, 128, N), F32),
            pltpu.VMEM((16, 128, 256), F32),
            pltpu.VMEM((2, DEV, 2, 2, 8, L), F32),
            pltpu.VMEM((2, DEV, 2, 2, 8, L), F32),
            pltpu.VMEM((A, 64, 256), F32),
            pltpu.VMEM((A, 32, 256), F32),
            pltpu.VMEM((2, DEV, 2, 8, L), F32),
            pltpu.VMEM((2, DEV, 2, 8, L), F32),
            pltpu.VMEM((16, 128, 256), F32),
            pltpu.SemaphoreType.DMA((5,)),
            pltpu.SemaphoreType.DMA((2, 4)),
            pltpu.SemaphoreType.DMA((2,)),
            pltpu.SemaphoreType.DMA((2,)),
            pltpu.SemaphoreType.DMA((2,)),
            pltpu.SemaphoreType.DMA((2, 16)),
            pltpu.SemaphoreType.DMA((16,)),
        ],
        compiler_params=pltpu.CompilerParams(
            collective_id=0, has_side_effects=True, vmem_limit_bytes=62 * 2**20
        ),
        name="main",
    )(
        weights, g1.reshape(128, N), g2.reshape(128, N),
        tab["twid"], tab["row"], tab["colf"], tab["coli"], tab["back"],
    )


def last_kernel(z_ref, out_ref):
    for j in range(ROWS // 8):
        rows = slice(8 * j, 8 * j + 8)
        X = [(z_ref[0, rows, 0:L], None)]
        X += [(z_ref[k, rows, 0:L], z_ref[k, rows, L : 2 * L]) for k in range(1, 16)]
        X += [(z_ref[0, rows, L : 2 * L], None)]
        for p, v in enumerate(irfft(X, A)):
            out_ref[rows, L * p : L * p + L] = v


def last_stage(z):
    return pl.pallas_call(
        last_kernel,
        grid=(STEPS,),
        in_specs=[pl.BlockSpec((16, ROWS, 256), lambda i: (0, i, 0))],
        out_specs=pl.BlockSpec((ROWS, N), lambda i: (i, 0)),
        out_shape=jax.ShapeDtypeStruct((128, N), F32),
        name="last",
    )(z)


def on_device(shear_one, shear_two, weights):
    tab = {k: jnp.asarray(v) for k, v in tables().items()}
    z = main_stage(shear_one, shear_two, weights, tab)
    return last_stage(z).reshape(1, 128, N)


def solution(mesh):
    spec = P("bin", "tile", None)
    return jax.shard_map(
        on_device, mesh=mesh, in_specs=(spec, spec, P()), out_specs=spec, check_vma=False
    )
```

```python
import functools

import jax
import jax.numpy as jnp
import ml_dtypes
import numpy as np
from jax import lax
from jax.experimental import pallas as pl
from jax.experimental.pallas import tpu as pltpu
from jax.sharding import PartitionSpec as P

N = 4096
A = 32
L = 128
DEV = 128
BINS = 4
F32 = jnp.float32
BF16 = jnp.bfloat16


def hi_lo(matrix):
    hi = matrix.astype(ml_dtypes.bfloat16)
    lo = (matrix - hi.astype(np.float64)).astype(ml_dtypes.bfloat16)
    return np.stack([hi, lo])


def tables():
    lane = np.arange(L)
    angle = 2.0 * np.pi * ((lane[:, None] * lane[None, :]) % L) / L
    c, s = np.cos(angle), np.sin(angle)
    fwd = np.block([[c, s], [-s, c]])
    slot = np.arange(64)
    a0 = 2.0 * np.pi * ((slot[:, None] * lane[None, :]) % L) / L
    a16 = 2.0 * np.pi * (((16 + 32 * slot[:, None]) * lane[None, :]) % N) / N
    first = np.zeros((256, 256))
    first[0:64, 0:128] = np.cos(a0)
    first[128:192, 0:128] = -np.sin(a0)
    first[128, 0:128] = (-1.0) ** lane
    first[64:128, 128:256] = np.cos(a16)
    first[192:256, 128:256] = -np.sin(a16)
    last = 2.0 * first.copy()
    last[0, 0:128] = 1.0
    last[128, 0:128] = (-1.0) ** lane
    k = np.arange(A)
    tw = 2.0 * np.pi * ((k[:, None] * lane[None, :]) % N) / N
    twid = np.stack([np.cos(tw), np.sin(tw)], 1).astype(np.float32)
    twid = np.broadcast_to(twid[:, :, None, :], (A, 2, 8, L)).copy()
    return dict(
        row=np.stack([hi_lo(first), hi_lo(fwd)]),
        colf=hi_lo(fwd.T),
        coli=hi_lo(fwd),
        back=np.stack(
            [
                np.stack([hi_lo(m.reshape(2, 2, 64, 256)[:, h].reshape(128, 256)) for h in range(2)])
                for m in (last, fwd)
            ]
        ),
        twid=twid,
    )


def fft(xs, sign):
    n = len(xs)
    if n == 1:
        return xs
    even, odd = fft(xs[0::2], sign), fft(xs[1::2], sign)
    out = [None] * n
    h = n // 2
    root = np.float32(np.sqrt(0.5))
    for k in range(h):
        er, ei = even[k]
        r, i = odd[k]
        if k == 0:
            tr, ti = r, i
        elif 4 * k == n:
            tr, ti = (-i, r) if sign > 0 else (i, -r)
            if sign > 0:
                out[k], out[k + h] = (er - i, ei + r), (er + i, ei - r)
            else:
                out[k], out[k + h] = (er + i, ei - r), (er - i, ei + r)
            continue
        elif 8 * k == n:
            tr, ti = ((r - i) * root, (r + i) * root) if sign > 0 else ((r + i) * root, (i - r) * root)
        elif 8 * k == 3 * n:
            if sign > 0:
                pr, pi = (r + i) * root, (r - i) * root
                out[k], out[k + h] = (er - pr, ei + pi), (er + pr, ei - pi)
            else:
                pr, pi = (i - r) * root, (r + i) * root
                out[k], out[k + h] = (er + pr, ei - pi), (er - pr, ei + pi)
            continue
        else:
            c = np.float32(np.cos(2 * np.pi * k / n))
            s = np.float32(sign * np.sin(2 * np.pi * k / n))
            tr, ti = r * c - i * s, r * s + i * c
        out[k], out[k + h] = (er + tr, ei + ti), (er - tr, ei - ti)
    return out


def rfft(xs):
    n = len(xs)
    if n == 2:
        return [(xs[0] + xs[1], None), (xs[0] - xs[1], None)]
    even, odd = rfft(xs[0::2]), rfft(xs[1::2])
    out = [None] * (n // 2 + 1)
    for k in range(n // 4 + 1):
        if k == 0:
            out[0] = (even[0][0] + odd[0][0], None)
            out[n // 2] = (even[0][0] - odd[0][0], None)
        elif 4 * k == n:
            out[k] = (even[k][0], -odd[k][0])
        else:
            er, ei = even[k]
            r, i = odd[k]
            if 8 * k == n:
                root = np.float32(np.sqrt(0.5))
                tr, ti = (r + i) * root, (i - r) * root
            else:
                c = np.float32(np.cos(2 * np.pi * k / n))
                s = np.float32(np.sin(2 * np.pi * k / n))
                tr, ti = r * c + i * s, i * c - r * s
            out[k] = (er + tr, ei + ti)
            out[n // 2 - k] = (er - tr, ti - ei)
    return out


def irfft(X, n):
    if n == 2:
        a, b = X[0][0], X[1][0]
        return [a + b, a - b]
    h = n // 2
    even, odd = [None] * (h // 2 + 1), [None] * (h // 2 + 1)
    for k in range(h // 2 + 1):
        if k == 0:
            even[0] = (X[0][0] + X[h][0], None)
            odd[0] = (X[0][0] - X[h][0], None)
        elif 2 * k == h:
            even[k] = (X[k][0] + X[k][0], None)
            odd[k] = (-(X[k][1] + X[k][1]), None)
        else:
            ar, ai = X[k]
            br, bi = X[h - k]
            even[k] = (ar + br, ai - bi)
            dr, di = ar - br, ai + bi
            if 4 * k == h:
                root = np.float32(np.sqrt(0.5))
                odd[k] = ((dr - di) * root, (dr + di) * root)
            else:
                c = np.float32(np.cos(2 * np.pi * k / n))
                s = np.float32(np.sin(2 * np.pi * k / n))
                odd[k] = (dr * c - di * s, dr * s + di * c)
    e, o = irfft(even, h), irfft(odd, h)
    out = [None] * n
    out[0::2] = e
    out[1::2] = o
    return out


def split(x):
    hi = x.astype(BF16)
    lo = (x - hi.astype(F32)).astype(BF16)
    return hi, lo


ROWS = 64
STEPS = 128 // ROWS
GROUP = 8
FLAT = pl.DeviceIdType.LOGICAL


def row_butterflies(comp, i, x_ref, tw_ref, y_ref):
    rows = pl.ds(pl.multiple_of(8 * i, 8), 8)
    X = rfft([x_ref[comp, rows, L * p : L * p + L] for p in range(A)])
    y_ref[0, rows, 0:L] = X[0][0]
    y_ref[0, rows, L : 2 * L] = X[16][0]
    for k in range(1, 16):
        r, m = X[k]
        c, s = tw_ref[k, 0], tw_ref[k, 1]
        y_ref[k, rows, 0:L] = r * c + m * s
        y_ref[k, rows, L : 2 * L] = m * c - r * s


def row_matmul(comp, k, w_ref, y_ref, send_ref):
    hi, lo = split(y_ref[k])
    sel = jnp.minimum(k, 1)
    whi, wlo = w_ref[sel, 0], w_ref[sel, 1]
    dims = (((1,), (1,)), ((), ()))
    dot = functools.partial(lax.dot_general, dimension_numbers=dims, preferred_element_type=F32)
    out = dot(whi, hi) + (dot(whi, lo) + dot(wlo, hi))
    for h in range(2):
        for c in range(2):
            for d in range(8):
                at = 128 * c + 64 * h + 8 * d
                send_ref[h, 8 * k + d, comp, c] = out[at : at + 8]


def col_forward(half, b, packed, x_ref, tw_ref, y_ref):
    lane = lax.broadcasted_iota(jnp.int32, (8, L), 1)
    sign = jnp.where(lane % 2 == 0, 1.0, -1.0).astype(F32)
    total = x_ref[half, A * b, 1, 1]
    for t in range(1, A):
        total = total + x_ref[half, A * b + t, 1, 1]
    corner = sign * (jnp.sum(total * sign, axis=1, keepdims=True) * np.float32(-1.0 / N))
    for R in range(2):
        xs = []
        for t in range(A):
            re = x_ref[half, A * b + t, R, 0]
            im = x_ref[half, A * b + t, R, 1]
            if R == 0:
                im = jnp.where(packed, corner, im)
            else:
                re = jnp.where(packed, 0.0, re)
                im = jnp.where(packed, x_ref[half, A * b + t, 0, 1], im)
            xs.append((re, im))
        X = fft(xs, -1)
        rows = pl.ds(pl.multiple_of(32 * R + 8 * b, 8), 8)
        for k in range(A):
            r, m = X[k]
            if k:
                c, s = tw_ref[k, 0], tw_ref[k, 1]
                r, m = r * c + m * s, m * c - r * s
            y_ref[k, rows, 0:L] = r
            y_ref[k, rows, L : 2 * L] = m


def col_middle(half, g, me, packed, w, tw_ref, wf_ref, wi_ref, y_ref, z_ref):
    base = g * GROUP
    group, part = me // 8, me % 8
    sub = lax.broadcasted_iota(jnp.int32, (8, L), 0)
    lane = lax.broadcasted_iota(jnp.int32, (8, L), 1)
    hi, lo = split(y_ref[pl.ds(base, GROUP)].reshape(GROUP * 64, 256))
    dot = functools.partial(jnp.dot, preferred_element_type=F32)
    G = dot(hi, wf_ref[0]) + (dot(lo, wf_ref[0]) + dot(hi, wf_ref[1]))
    at = 8 * part + sub
    col = jnp.where(group == 0, 32 * at + 16 * half, group + 32 * (64 * half + at))
    col = jnp.where(col < N // 2, col, col - N).astype(F32)
    rows = []
    for kk in range(GROUP):
        u = base + kk + A * lane
        nyquist = u == N // 2
        row = jnp.where(u < N // 2, u, u - N).astype(F32)
        row2 = row * row

        def kern(l1):
            q = jnp.maximum(l1 * l1 + row2, 1.0)
            return (l1 * l1 - row2) / q, (2.0 * l1) * row / q

        a, b = kern(col)
        ar, ai = a, jnp.where(nyquist, -b, 0.0)
        a2, b2 = kern(np.float32(-N // 2))
        br = jnp.where(packed, a2, jnp.where(nyquist, 0.0, b))
        bi = jnp.where(jnp.logical_and(packed, jnp.logical_not(nyquist)), -b2, 0.0)
        H = []
        for b_ in range(BINS):
            o1, o2 = kk * 64 + 8 * b_, kk * 64 + 32 + 8 * b_
            g1r, g1i = G[o1 : o1 + 8, 0:L], G[o1 : o1 + 8, L : 2 * L]
            g2r, g2i = G[o2 : o2 + 8, 0:L], G[o2 : o2 + 8, L : 2 * L]
            hr = ar * g1r - ai * g1i + br * g2r - bi * g2i
            hm = ar * g1i + ai * g1r + br * g2i + bi * g2r
            H.append((hr, hm))
        for j in range(BINS):
            fr, fi = H[0][0] * w[j][0], H[0][1] * w[j][0]
            for b_ in range(1, j + 1):
                fr, fi = fr + H[b_][0] * w[j][b_], fi + H[b_][1] * w[j][b_]
            rows.append(jnp.concatenate([fr, fi], axis=1))
    hi, lo = split(jnp.concatenate(rows, axis=0))
    Z = dot(hi, wi_ref[0]) + (dot(lo, wi_ref[0]) + dot(hi, wi_ref[1]))
    for kk in range(GROUP):
        c, s = tw_ref[base + kk, 0], tw_ref[base + kk, 1]
        for j in range(BINS):
            o = 32 * kk + 8 * j
            r, m = Z[o : o + 8, 0:L], Z[o : o + 8, L : 2 * L]
            z_ref[base + kk, 8 * j : 8 * j + 8, 0:L] = r * c - m * s
            z_ref[base + kk, 8 * j : 8 * j + 8, L : 2 * L] = m * c + r * s


def col_inverse(half, j, z_ref, ret_ref):
    rows = pl.ds(pl.multiple_of(8 * j, 8), 8)
    xs = [(z_ref[k, rows, 0:L], z_ref[k, rows, L : 2 * L]) for k in range(A)]
    for t, (r, m) in enumerate(fft(xs, 1)):
        ret_ref[half, A * j + t, 0] = r
        ret_ref[half, A * j + t, 1] = m


def back_matmul(half, k, in_ref, w_ref):
    parts = [in_ref[half, 8 * k + d, c] for c in range(2) for d in range(8)]
    hi, lo = split(jnp.concatenate(parts, axis=0).T)
    sel = jnp.minimum(k, 1)
    dot = functools.partial(jnp.dot, preferred_element_type=F32)
    whi, wlo = w_ref[sel, half, 0], w_ref[sel, half, 1]
    return dot(hi, whi) + (dot(lo, whi) + dot(hi, wlo))


def back_twiddle(k, Z, tw_ref, z_ref):
    c, s = tw_ref[k, 0, 0:1], tw_ref[k, 1, 0:1]
    r, m = Z[:, 0:L], Z[:, L : 2 * L]
    z_ref[k, :, 0:L] = r * c - m * s
    z_ref[k, :, L : 2 * L] = m * c + r * s


def main_kernel(
    wgt_ref, g1_ref, g2_ref, tw_any, wr_any, wf_any, wi_any, wb_any, out_ref,
    tw_ref, wr_ref, wf_ref, wi_ref, wb_ref,
    x_ref, yr_ref, send_ref, recv_ref, y_ref, z_ref, ret_ref, land_ref, last_ref,
    tab_sem, in_sem, go_send, go_recv, ret_send, ret_recv, out_sem,
):
    mybin, mytile = lax.axis_index("bin"), lax.axis_index("tile")
    me = mybin * 32 + mytile
    myz, myx = lax.div(mytile, 8), lax.rem(lax.div(mytile, 2), 4)
    myy = 2 * lax.rem(mytile, 2) + lax.div(mybin, 2)
    mycore = lax.rem(mybin, 2)
    mygroup = 8 * lax.rem(myz, 2) + 4 * lax.rem(myx, 2) + mybin
    mysid = 8 * mygroup + 4 * lax.div(myz, 2) + 2 * lax.div(myx, 2) + lax.rem(mytile, 2)

    def group_at(i):
        og = jnp.where(lax.rem(i, 2) == 0, 15 - lax.div(i, 2), lax.div(i, 2))
        zb = myz + lax.div(og, 8)
        xb = myx + lax.rem(lax.div(og, 4), 2)
        yb = myy + lax.rem(lax.div(og, 2), 2)
        core = lax.rem(mycore + og, 2)
        k = 8 * lax.rem(zb, 2) + 4 * lax.rem(xb, 2) + 2 * lax.rem(yb, 2) + core
        z = [lax.rem(zb + 2 * p, 4) for p in range(2)]
        x = [lax.rem(xb + 2 * p, 4) for p in range(2)]
        y = [lax.rem(yb + 2 * p, 4) for p in range(2)]
        base = 32 * core + 64 * lax.rem(yb, 2)
        targets = []
        for p in (0, 7, 1, 6, 2, 5, 4, 3):
            pz, px, py = z[p // 4], x[p // 2 % 2], y[p % 2]
            sid = 8 * k + 4 * lax.div(pz, 2) + 2 * lax.div(px, 2) + lax.div(py, 2)
            targets.append((sid, base + 8 * pz + 2 * px + lax.div(py, 2)))
        return og, k, targets

    barrier = pltpu.get_barrier_semaphore()

    def greet(i, carry):
        pl.semaphore_signal(
            barrier, inc=1, device_id=lax.rem(me + i, DEV), device_id_type=FLAT
        )
        return carry

    tabs = [
        pltpu.make_async_copy(a, b, tab_sem.at[i])
        for i, (a, b) in enumerate(
            zip((tw_any, wr_any, wf_any, wi_any, wb_any), (tw_ref, wr_ref, wf_ref, wi_ref, wb_ref))
        )
    ]

    def load(comp, i):
        rows = pl.ds(pl.multiple_of(32 * i, 32), 32)
        return pltpu.make_async_copy(
            (g1_ref, g2_ref)[comp].at[rows], x_ref.at[comp, rows], in_sem.at[comp, i]
        )

    tabs[0].start()
    for i in range(4):
        load(0, i).start()
    tabs[1].start()
    for i in range(4):
        load(1, i).start()
    for t in tabs[2:]:
        t.start()
    lax.fori_loop(1, DEV, greet, 0)
    tabs[0].wait()

    def go(half, sid, dest, comp):
        at = (half, sid) if comp is None else (half, sid, comp)
        to = (half, me) if comp is None else (half, me, comp)
        pltpu.make_async_remote_copy(
            src_ref=send_ref.at[at],
            dst_ref=recv_ref.at[to],
            send_sem=go_send.at[half],
            recv_sem=go_recv.at[half],
            device_id=dest,
            device_id_type=FLAT,
        ).start()

    def rows_of(comp):
        def some_rows(i, carry):
            load(comp, i).wait()

            def step(j, c):
                row_butterflies(comp, 4 * i + j, x_ref, tw_ref, yr_ref)
                return c

            return lax.fori_loop(0, 4, step, carry)

        def matmul_step(i, carry):
            og, k, targets = group_at(i)
            row_matmul(comp, k, wr_ref, yr_ref, send_ref)

            @pl.when(og > 0)
            def _():
                go(0, *targets[0], comp)

            for sid, dest in targets[1:]:
                go(0, sid, dest, comp)
            return carry

        lax.fori_loop(0, 4, some_rows, 0)
        if comp == 0:
            tabs[1].wait()
            pl.semaphore_wait(barrier, DEV - 1)
        lax.fori_loop(0, 16, matmul_step, 0)

    rows_of(0)
    rows_of(1)
    for half in range(2):
        pltpu.make_async_copy(
            send_ref.at[half, mysid], recv_ref.at[half, me], go_recv.at[half]
        ).start()

    def second(i, carry):
        og, _, targets = group_at(i)

        @pl.when(og > 0)
        def _():
            go(1, *targets[0], None)

        for sid, dest in targets[1:]:
            go(1, sid, dest, None)
        return carry

    lax.fori_loop(0, 16, second, 0)
    for t in tabs[2:]:
        t.wait()

    sub = lax.broadcasted_iota(jnp.int32, (8, L), 0)
    scale = np.float32(1.0 / (N * N))
    w = [[wgt_ref[j, b] * scale for b in range(j + 1)] for j in range(BINS)]

    def half_step(half, carry):
        packed = jnp.logical_and(sub == 0, jnp.logical_and(mysid == 0, half == 0))
        pltpu.make_async_copy(send_ref.at[half], recv_ref.at[half], go_recv.at[half]).wait()

        def forward(b, c):
            col_forward(half, b, packed, recv_ref, tw_ref, y_ref)
            return c

        def middle(g, c):
            col_middle(half, g, mysid, packed, w, tw_ref, wf_ref, wi_ref, y_ref, z_ref)
            return c

        def inverse(i, c):
            j = lax.rem(mybin + i, BINS)
            col_inverse(half, j, z_ref, ret_ref)

            def ret(dest):
                pltpu.make_async_remote_copy(
                    src_ref=ret_ref.at[half, dest],
                    dst_ref=land_ref.at[half, mysid],
                    send_sem=ret_send.at[half],
                    recv_sem=ret_recv.at[half, mygroup],
                    device_id=dest,
                    device_id_type=FLAT,
                ).start()

            def ret_step(q, c2):
                zb, xb = myz + lax.div(q, 2), myx + lax.rem(q, 2)
                z = [lax.rem(zb + 2 * p, 4) for p in range(2)]
                x = [lax.rem(xb + 2 * p, 4) for p in range(2)]
                h = [lax.rem(mytile + p, 2) for p in range(2)]

                @pl.when(i + q > 0)
                def _():
                    ret(32 * j + 8 * z[0] + 2 * x[0] + h[0])

                for p in (7, 1, 6, 2, 5, 4, 3):
                    ret(32 * j + 8 * z[p // 4] + 2 * x[p // 2 % 2] + h[p % 2])
                return c2

            return lax.fori_loop(0, 4, ret_step, c)

        lax.fori_loop(0, BINS, forward, 0)
        lax.fori_loop(0, A // GROUP, middle, 0)
        lax.fori_loop(0, BINS, inverse, 0)
        pltpu.make_async_copy(
            ret_ref.at[half, me], land_ref.at[half, mysid], ret_recv.at[half, mygroup]
        ).start()
        return carry

    lax.fori_loop(0, 2, half_step, 0)

    def write(k):
        return pltpu.make_async_copy(last_ref.at[k], out_ref.at[k], out_sem.at[k])

    def back_of(half):
        def back_step(i, carry):
            b = lax.rem(mybin + 4 - lax.div(i, 4), 4)
            q = lax.rem(i, 4)
            k = 8 * lax.rem(myz + lax.div(q, 2), 2) + 4 * lax.rem(myx + q, 2) + b
            eight = pl.ds(pl.multiple_of(8 * k, 8), 8)
            pltpu.make_async_copy(
                ret_ref.at[half, eight], land_ref.at[half, eight], ret_recv.at[half, k]
            ).wait()
            Z = back_matmul(half, k, land_ref, wb_ref)
            if half == 0:
                last_ref[k] = Z
            else:
                back_twiddle(k, last_ref[k] + Z, tw_ref, last_ref)
                write(k).start()
            return carry

        lax.fori_loop(0, 16, back_step, 0)

    back_of(0)
    back_of(1)

    def finish(half, carry):
        for src, sem in ((send_ref, go_send), (ret_ref, ret_send)):
            part = src.at[half, pl.ds(0, DEV - 1)]
            pltpu.make_async_remote_copy(
                src_ref=part, dst_ref=part, send_sem=sem.at[half], recv_sem=sem.at[half],
                device_id=me, device_id_type=FLAT,
            ).wait_send()
        return carry

    lax.fori_loop(0, 2, finish, 0)

    def written(k, carry):
        write(k).wait()
        return carry

    lax.fori_loop(0, 16, written, 0)


def main_stage(g1, g2, weights, tab):
    hbm = pl.BlockSpec(memory_space=pl.ANY)
    return pl.pallas_call(
        main_kernel,
        in_specs=[pl.BlockSpec(memory_space=pltpu.SMEM)] + [hbm] * 7,
        out_specs=hbm,
        out_shape=jax.ShapeDtypeStruct((16, 128, 256), F32),
        scratch_shapes=[
            pltpu.VMEM((A, 2, 8, L), F32),
            pltpu.VMEM((2, 2, 256, 256), BF16),
            pltpu.VMEM((2, 256, 256), BF16),
            pltpu.VMEM((2, 256, 256), BF16),
            pltpu.VMEM((2, 2, 2, 128, 256), BF16),
            pltpu.VMEM((2, 128, N), F32),
            pltpu.VMEM((16, 128, 256), F32),
            pltpu.VMEM((2, DEV, 2, 2, 8, L), F32),
            pltpu.VMEM((2, DEV, 2, 2, 8, L), F32),
            pltpu.VMEM((A, 64, 256), F32),
            pltpu.VMEM((A, 32, 256), F32),
            pltpu.VMEM((2, DEV, 2, 8, L), F32),
            pltpu.VMEM((2, DEV, 2, 8, L), F32),
            pltpu.VMEM((16, 128, 256), F32),
            pltpu.SemaphoreType.DMA((5,)),
            pltpu.SemaphoreType.DMA((2, 4)),
            pltpu.SemaphoreType.DMA((2,)),
            pltpu.SemaphoreType.DMA((2,)),
            pltpu.SemaphoreType.DMA((2,)),
            pltpu.SemaphoreType.DMA((2, 16)),
            pltpu.SemaphoreType.DMA((16,)),
        ],
        compiler_params=pltpu.CompilerParams(
            collective_id=0, has_side_effects=True, vmem_limit_bytes=62 * 2**20
        ),
        name="main",
    )(
        weights, g1.reshape(128, N), g2.reshape(128, N),
        tab["twid"], tab["row"], tab["colf"], tab["coli"], tab["back"],
    )


def last_kernel(z_ref, out_ref):
    for j in range(ROWS // 8):
        rows = slice(8 * j, 8 * j + 8)
        X = [(z_ref[0, rows, 0:L], None)]
        X += [(z_ref[k, rows, 0:L], z_ref[k, rows, L : 2 * L]) for k in range(1, 16)]
        X += [(z_ref[0, rows, L : 2 * L], None)]
        for p, v in enumerate(irfft(X, A)):
            out_ref[rows, L * p : L * p + L] = v


def last_stage(z):
    return pl.pallas_call(
        last_kernel,
        grid=(STEPS,),
        in_specs=[pl.BlockSpec((16, ROWS, 256), lambda i: (0, i, 0))],
        out_specs=pl.BlockSpec((ROWS, N), lambda i: (i, 0)),
        out_shape=jax.ShapeDtypeStruct((128, N), F32),
        name="last",
    )(z)


def on_device(shear_one, shear_two, weights):
    tab = {k: jnp.asarray(v) for k, v in tables().items()}
    z = main_stage(shear_one, shear_two, weights, tab)
    return last_stage(z).reshape(1, 128, N)


def solution(mesh):
    spec = P("bin", "tile", None)
    return jax.shard_map(
        on_device, mesh=mesh, in_specs=(spec, spec, P()), out_specs=spec, check_vma=False
    )
```

```python
import functools

import jax
import jax.numpy as jnp
import ml_dtypes
import numpy as np
from jax import lax
from jax.experimental import pallas as pl
from jax.experimental.pallas import tpu as pltpu
from jax.sharding import PartitionSpec as P

N = 4096
A = 32
L = 128
DEV = 128
BINS = 4
F32 = jnp.float32
BF16 = jnp.bfloat16


def hi_lo(matrix):
    hi = matrix.astype(ml_dtypes.bfloat16)
    lo = (matrix - hi.astype(np.float64)).astype(ml_dtypes.bfloat16)
    return np.stack([hi, lo])


def tables():
    lane = np.arange(L)
    angle = 2.0 * np.pi * ((lane[:, None] * lane[None, :]) % L) / L
    c, s = np.cos(angle), np.sin(angle)
    fwd = np.block([[c, s], [-s, c]])
    slot = np.arange(64)
    a0 = 2.0 * np.pi * ((slot[:, None] * lane[None, :]) % L) / L
    a16 = 2.0 * np.pi * (((16 + 32 * slot[:, None]) * lane[None, :]) % N) / N
    first = np.zeros((256, 256))
    first[0:64, 0:128] = np.cos(a0)
    first[128:192, 0:128] = -np.sin(a0)
    first[128, 0:128] = (-1.0) ** lane
    first[64:128, 128:256] = np.cos(a16)
    first[192:256, 128:256] = -np.sin(a16)
    last = 2.0 * first.copy()
    last[0, 0:128] = 1.0
    last[128, 0:128] = (-1.0) ** lane
    k = np.arange(A)
    tw = 2.0 * np.pi * ((k[:, None] * lane[None, :]) % N) / N
    twid = np.stack([np.cos(tw), np.sin(tw)], 1).astype(np.float32)
    twid = np.broadcast_to(twid[:, :, None, :], (A, 2, 8, L)).copy()
    return dict(
        row=np.stack([hi_lo(first), hi_lo(fwd)]),
        colf=hi_lo(fwd.T),
        coli=hi_lo(fwd),
        back=np.stack(
            [
                np.stack([hi_lo(m.reshape(2, 2, 64, 256)[:, h].reshape(128, 256)) for h in range(2)])
                for m in (last, fwd)
            ]
        ),
        twid=twid,
    )


def fft(xs, sign):
    n = len(xs)
    if n == 1:
        return xs
    even, odd = fft(xs[0::2], sign), fft(xs[1::2], sign)
    out = [None] * n
    h = n // 2
    root = np.float32(np.sqrt(0.5))
    for k in range(h):
        er, ei = even[k]
        r, i = odd[k]
        if k == 0:
            tr, ti = r, i
        elif 4 * k == n:
            tr, ti = (-i, r) if sign > 0 else (i, -r)
            if sign > 0:
                out[k], out[k + h] = (er - i, ei + r), (er + i, ei - r)
            else:
                out[k], out[k + h] = (er + i, ei - r), (er - i, ei + r)
            continue
        elif 8 * k == n:
            tr, ti = ((r - i) * root, (r + i) * root) if sign > 0 else ((r + i) * root, (i - r) * root)
        elif 8 * k == 3 * n:
            if sign > 0:
                pr, pi = (r + i) * root, (r - i) * root
                out[k], out[k + h] = (er - pr, ei + pi), (er + pr, ei - pi)
            else:
                pr, pi = (i - r) * root, (r + i) * root
                out[k], out[k + h] = (er + pr, ei - pi), (er - pr, ei + pi)
            continue
        else:
            c = np.float32(np.cos(2 * np.pi * k / n))
            s = np.float32(sign * np.sin(2 * np.pi * k / n))
            tr, ti = r * c - i * s, r * s + i * c
        out[k], out[k + h] = (er + tr, ei + ti), (er - tr, ei - ti)
    return out


def rfft(xs):
    n = len(xs)
    if n == 2:
        return [(xs[0] + xs[1], None), (xs[0] - xs[1], None)]
    even, odd = rfft(xs[0::2]), rfft(xs[1::2])
    out = [None] * (n // 2 + 1)
    for k in range(n // 4 + 1):
        if k == 0:
            out[0] = (even[0][0] + odd[0][0], None)
            out[n // 2] = (even[0][0] - odd[0][0], None)
        elif 4 * k == n:
            out[k] = (even[k][0], -odd[k][0])
        else:
            er, ei = even[k]
            r, i = odd[k]
            if 8 * k == n:
                root = np.float32(np.sqrt(0.5))
                tr, ti = (r + i) * root, (i - r) * root
            else:
                c = np.float32(np.cos(2 * np.pi * k / n))
                s = np.float32(np.sin(2 * np.pi * k / n))
                tr, ti = r * c + i * s, i * c - r * s
            out[k] = (er + tr, ei + ti)
            out[n // 2 - k] = (er - tr, ti - ei)
    return out


def irfft(X, n):
    if n == 2:
        a, b = X[0][0], X[1][0]
        return [a + b, a - b]
    h = n // 2
    even, odd = [None] * (h // 2 + 1), [None] * (h // 2 + 1)
    for k in range(h // 2 + 1):
        if k == 0:
            even[0] = (X[0][0] + X[h][0], None)
            odd[0] = (X[0][0] - X[h][0], None)
        elif 2 * k == h:
            even[k] = (X[k][0] + X[k][0], None)
            odd[k] = (-(X[k][1] + X[k][1]), None)
        else:
            ar, ai = X[k]
            br, bi = X[h - k]
            even[k] = (ar + br, ai - bi)
            dr, di = ar - br, ai + bi
            if 4 * k == h:
                root = np.float32(np.sqrt(0.5))
                odd[k] = ((dr - di) * root, (dr + di) * root)
            else:
                c = np.float32(np.cos(2 * np.pi * k / n))
                s = np.float32(np.sin(2 * np.pi * k / n))
                odd[k] = (dr * c - di * s, dr * s + di * c)
    e, o = irfft(even, h), irfft(odd, h)
    out = [None] * n
    out[0::2] = e
    out[1::2] = o
    return out


def split(x):
    hi = x.astype(BF16)
    lo = (x - hi.astype(F32)).astype(BF16)
    return hi, lo


ROWS = 64
STEPS = 128 // ROWS
GROUP = 8
FLAT = pl.DeviceIdType.LOGICAL


def row_butterflies(comp, i, x_ref, tw_ref, y_ref):
    rows = pl.ds(pl.multiple_of(8 * i, 8), 8)
    X = rfft([x_ref[comp, rows, L * p : L * p + L] for p in range(A)])
    y_ref[0, rows, 0:L] = X[0][0]
    y_ref[0, rows, L : 2 * L] = X[16][0]
    for k in range(1, 16):
        r, m = X[k]
        c, s = tw_ref[k, 0], tw_ref[k, 1]
        y_ref[k, rows, 0:L] = r * c + m * s
        y_ref[k, rows, L : 2 * L] = m * c - r * s


def row_matmul(comp, k, w_ref, y_ref, send_ref):
    hi, lo = split(y_ref[k])
    sel = jnp.minimum(k, 1)
    whi, wlo = w_ref[sel, 0], w_ref[sel, 1]
    dims = (((1,), (1,)), ((), ()))
    dot = functools.partial(lax.dot_general, dimension_numbers=dims, preferred_element_type=F32)
    out = dot(whi, hi) + (dot(whi, lo) + dot(wlo, hi))
    for h in range(2):
        for c in range(2):
            for d in range(8):
                at = 128 * c + 64 * h + 8 * d
                send_ref[h, 8 * k + d, comp, c] = out[at : at + 8]


def col_forward(half, b, packed, x_ref, tw_ref, y_ref):
    lane = lax.broadcasted_iota(jnp.int32, (8, L), 1)
    sign = jnp.where(lane % 2 == 0, 1.0, -1.0).astype(F32)
    total = x_ref[half, A * b, 1, 1]
    for t in range(1, A):
        total = total + x_ref[half, A * b + t, 1, 1]
    corner = sign * (jnp.sum(total * sign, axis=1, keepdims=True) * np.float32(-1.0 / N))
    for R in range(2):
        xs = []
        for t in range(A):
            re = x_ref[half, A * b + t, R, 0]
            im = x_ref[half, A * b + t, R, 1]
            if R == 0:
                im = jnp.where(packed, corner, im)
            else:
                re = jnp.where(packed, 0.0, re)
                im = jnp.where(packed, x_ref[half, A * b + t, 0, 1], im)
            xs.append((re, im))
        X = fft(xs, -1)
        rows = pl.ds(pl.multiple_of(32 * R + 8 * b, 8), 8)
        for k in range(A):
            r, m = X[k]
            if k:
                c, s = tw_ref[k, 0], tw_ref[k, 1]
                r, m = r * c + m * s, m * c - r * s
            y_ref[k, rows, 0:L] = r
            y_ref[k, rows, L : 2 * L] = m


def col_middle(half, g, me, packed, w, tw_ref, wf_ref, wi_ref, y_ref, z_ref):
    base = g * GROUP
    group, part = me // 8, me % 8
    sub = lax.broadcasted_iota(jnp.int32, (8, L), 0)
    lane = lax.broadcasted_iota(jnp.int32, (8, L), 1)
    hi, lo = split(y_ref[pl.ds(base, GROUP)].reshape(GROUP * 64, 256))
    dot = functools.partial(jnp.dot, preferred_element_type=F32)
    G = dot(hi, wf_ref[0]) + (dot(lo, wf_ref[0]) + dot(hi, wf_ref[1]))
    at = 8 * part + sub
    col = jnp.where(group == 0, 32 * at + 16 * half, group + 32 * (64 * half + at))
    col = jnp.where(col < N // 2, col, col - N).astype(F32)
    rows = []
    for kk in range(GROUP):
        u = base + kk + A * lane
        nyquist = u == N // 2
        row = jnp.where(u < N // 2, u, u - N).astype(F32)
        row2 = row * row

        def kern(l1):
            q = jnp.maximum(l1 * l1 + row2, 1.0)
            return (l1 * l1 - row2) / q, (2.0 * l1) * row / q

        a, b = kern(col)
        ar, ai = a, jnp.where(nyquist, -b, 0.0)
        a2, b2 = kern(np.float32(-N // 2))
        br = jnp.where(packed, a2, jnp.where(nyquist, 0.0, b))
        bi = jnp.where(jnp.logical_and(packed, jnp.logical_not(nyquist)), -b2, 0.0)
        H = []
        for b_ in range(BINS):
            o1, o2 = kk * 64 + 8 * b_, kk * 64 + 32 + 8 * b_
            g1r, g1i = G[o1 : o1 + 8, 0:L], G[o1 : o1 + 8, L : 2 * L]
            g2r, g2i = G[o2 : o2 + 8, 0:L], G[o2 : o2 + 8, L : 2 * L]
            hr = ar * g1r - ai * g1i + br * g2r - bi * g2i
            hm = ar * g1i + ai * g1r + br * g2i + bi * g2r
            H.append((hr, hm))
        for j in range(BINS):
            fr, fi = H[0][0] * w[j][0], H[0][1] * w[j][0]
            for b_ in range(1, j + 1):
                fr, fi = fr + H[b_][0] * w[j][b_], fi + H[b_][1] * w[j][b_]
            rows.append(jnp.concatenate([fr, fi], axis=1))
    hi, lo = split(jnp.concatenate(rows, axis=0))
    Z = dot(hi, wi_ref[0]) + (dot(lo, wi_ref[0]) + dot(hi, wi_ref[1]))
    for kk in range(GROUP):
        c, s = tw_ref[base + kk, 0], tw_ref[base + kk, 1]
        for j in range(BINS):
            o = 32 * kk + 8 * j
            r, m = Z[o : o + 8, 0:L], Z[o : o + 8, L : 2 * L]
            z_ref[base + kk, 8 * j : 8 * j + 8, 0:L] = r * c - m * s
            z_ref[base + kk, 8 * j : 8 * j + 8, L : 2 * L] = m * c + r * s


def col_inverse(half, j, z_ref, ret_ref):
    rows = pl.ds(pl.multiple_of(8 * j, 8), 8)
    xs = [(z_ref[k, rows, 0:L], z_ref[k, rows, L : 2 * L]) for k in range(A)]
    for t, (r, m) in enumerate(fft(xs, 1)):
        ret_ref[half, A * j + t, 0] = r
        ret_ref[half, A * j + t, 1] = m


def back_matmul(half, k, in_ref, w_ref):
    parts = [in_ref[half, 8 * k + d, c] for c in range(2) for d in range(8)]
    hi, lo = split(jnp.concatenate(parts, axis=0).T)
    sel = jnp.minimum(k, 1)
    dot = functools.partial(jnp.dot, preferred_element_type=F32)
    whi, wlo = w_ref[sel, half, 0], w_ref[sel, half, 1]
    return dot(hi, whi) + (dot(lo, whi) + dot(hi, wlo))


def back_twiddle(k, Z, tw_ref, z_ref):
    c, s = tw_ref[k, 0, 0:1], tw_ref[k, 1, 0:1]
    r, m = Z[:, 0:L], Z[:, L : 2 * L]
    z_ref[k, :, 0:L] = r * c - m * s
    z_ref[k, :, L : 2 * L] = m * c + r * s


def main_kernel(
    wgt_ref, g1_ref, g2_ref, tw_any, wr_any, wf_any, wi_any, wb_any, out_ref,
    tw_ref, wr_ref, wf_ref, wi_ref, wb_ref,
    x_ref, yr_ref, send_ref, recv_ref, y_ref, z_ref, ret_ref, land_ref, last_ref,
    tab_sem, in_sem, go_send, go_recv, ret_send, ret_recv, out_sem,
):
    mybin, mytile = lax.axis_index("bin"), lax.axis_index("tile")
    me = mybin * 32 + mytile
    myz, myx = lax.div(mytile, 8), lax.rem(lax.div(mytile, 2), 4)
    myy = 2 * lax.rem(mytile, 2) + lax.div(mybin, 2)
    mycore = lax.rem(mybin, 2)
    mygroup = 8 * lax.rem(myz, 2) + 4 * lax.rem(myx, 2) + mybin
    mysid = 8 * mygroup + 4 * lax.div(myz, 2) + 2 * lax.div(myx, 2) + lax.rem(mytile, 2)

    def group_at(i):
        og = jnp.where(lax.rem(i, 2) == 0, 15 - lax.div(i, 2), lax.div(i, 2))
        zb = myz + lax.div(og, 8)
        xb = myx + lax.rem(lax.div(og, 4), 2)
        yb = myy + lax.rem(lax.div(og, 2), 2)
        core = lax.rem(mycore + og, 2)
        k = 8 * lax.rem(zb, 2) + 4 * lax.rem(xb, 2) + 2 * lax.rem(yb, 2) + core
        z = [lax.rem(zb + 2 * p, 4) for p in range(2)]
        x = [lax.rem(xb + 2 * p, 4) for p in range(2)]
        y = [lax.rem(yb + 2 * p, 4) for p in range(2)]
        base = 32 * core + 64 * lax.rem(yb, 2)
        targets = []
        for p in (0, 7, 1, 6, 2, 5, 4, 3):
            pz, px, py = z[p // 4], x[p // 2 % 2], y[p % 2]
            sid = 8 * k + 4 * lax.div(pz, 2) + 2 * lax.div(px, 2) + lax.div(py, 2)
            targets.append((sid, base + 8 * pz + 2 * px + lax.div(py, 2)))
        return og, k, targets

    barrier = pltpu.get_barrier_semaphore()

    def greet(q, carry):
        core, h = lax.rem(mybin + q, 2), lax.div(mybin, 2)
        xs = [2 * lax.rem(myx + o, 4) for o in (2, 1, 3, 0)]
        y = lax.rem(myy + 2 + lax.div(q, 2), 4)
        base = 64 * lax.rem(y, 2) + 32 * core + lax.div(y, 2)
        for oz in (2, 1, 3, 0):
            z = 8 * lax.rem(myz + oz, 4)
            for x in xs:
                dest = base + z + x

                @pl.when(dest != me)
                def _():
                    pl.semaphore_signal(barrier, inc=1, device_id=dest, device_id_type=FLAT)

        return carry

    tabs = [
        pltpu.make_async_copy(a, b, tab_sem.at[i])
        for i, (a, b) in enumerate(
            zip((tw_any, wr_any, wf_any, wi_any, wb_any), (tw_ref, wr_ref, wf_ref, wi_ref, wb_ref))
        )
    ]

    def load(comp, i):
        rows = pl.ds(pl.multiple_of(32 * i, 32), 32)
        return pltpu.make_async_copy(
            (g1_ref, g2_ref)[comp].at[rows], x_ref.at[comp, rows], in_sem.at[comp, i]
        )

    tabs[0].start()
    for i in range(4):
        load(0, i).start()
    tabs[1].start()
    for i in range(4):
        load(1, i).start()
    for t in tabs[2:]:
        t.start()
    lax.fori_loop(0, 8, greet, 0)
    tabs[0].wait()

    def go(half, sid, dest, comp):
        at = (half, sid) if comp is None else (half, sid, comp)
        to = (half, me) if comp is None else (half, me, comp)
        pltpu.make_async_remote_copy(
            src_ref=send_ref.at[at],
            dst_ref=recv_ref.at[to],
            send_sem=go_send.at[half],
            recv_sem=go_recv.at[half],
            device_id=dest,
            device_id_type=FLAT,
        ).start()

    def rows_of(comp):
        def some_rows(i, carry):
            load(comp, i).wait()

            def step(j, c):
                row_butterflies(comp, 4 * i + j, x_ref, tw_ref, yr_ref)
                return c

            return lax.fori_loop(0, 4, step, carry)

        def matmul_step(i, carry):
            og, k, targets = group_at(i)
            row_matmul(comp, k, wr_ref, yr_ref, send_ref)

            @pl.when(og > 0)
            def _():
                go(0, *targets[0], comp)

            for sid, dest in targets[1:]:
                go(0, sid, dest, comp)
            return carry

        lax.fori_loop(0, 4, some_rows, 0)
        if comp == 0:
            tabs[1].wait()
            pl.semaphore_wait(barrier, DEV - 1)
        lax.fori_loop(0, 16, matmul_step, 0)

    rows_of(0)
    rows_of(1)
    for half in range(2):
        pltpu.make_async_copy(
            send_ref.at[half, mysid], recv_ref.at[half, me], go_recv.at[half]
        ).start()

    def second(i, carry):
        og, _, targets = group_at(i)

        @pl.when(og > 0)
        def _():
            go(1, *targets[0], None)

        for sid, dest in targets[1:]:
            go(1, sid, dest, None)
        return carry

    lax.fori_loop(0, 16, second, 0)
    for t in tabs[2:]:
        t.wait()

    sub = lax.broadcasted_iota(jnp.int32, (8, L), 0)
    scale = np.float32(1.0 / (N * N))
    w = [[wgt_ref[j, b] * scale for b in range(j + 1)] for j in range(BINS)]

    def half_step(half, carry):
        packed = jnp.logical_and(sub == 0, jnp.logical_and(mysid == 0, half == 0))
        pltpu.make_async_copy(send_ref.at[half], recv_ref.at[half], go_recv.at[half]).wait()

        def forward(b, c):
            col_forward(half, b, packed, recv_ref, tw_ref, y_ref)
            return c

        def middle(g, c):
            col_middle(half, g, mysid, packed, w, tw_ref, wf_ref, wi_ref, y_ref, z_ref)
            return c

        def inverse(i, c):
            j = lax.rem(mybin + i, BINS)
            col_inverse(half, j, z_ref, ret_ref)

            def ret(dest):
                pltpu.make_async_remote_copy(
                    src_ref=ret_ref.at[half, dest],
                    dst_ref=land_ref.at[half, mysid],
                    send_sem=ret_send.at[half],
                    recv_sem=ret_recv.at[half, mygroup],
                    device_id=dest,
                    device_id_type=FLAT,
                ).start()

            def ret_step(q, c2):
                zb, xb = myz + lax.div(q, 2), myx + lax.rem(q, 2)
                z = [lax.rem(zb + 2 * p, 4) for p in range(2)]
                x = [lax.rem(xb + 2 * p, 4) for p in range(2)]
                h = [lax.rem(mytile + p, 2) for p in range(2)]

                @pl.when(i + q > 0)
                def _():
                    ret(32 * j + 8 * z[0] + 2 * x[0] + h[0])

                for p in (7, 1, 6, 2, 5, 4, 3):
                    ret(32 * j + 8 * z[p // 4] + 2 * x[p // 2 % 2] + h[p % 2])
                return c2

            return lax.fori_loop(0, 4, ret_step, c)

        lax.fori_loop(0, BINS, forward, 0)
        lax.fori_loop(0, A // GROUP, middle, 0)
        lax.fori_loop(0, BINS, inverse, 0)
        pltpu.make_async_copy(
            ret_ref.at[half, me], land_ref.at[half, mysid], ret_recv.at[half, mygroup]
        ).start()
        return carry

    lax.fori_loop(0, 2, half_step, 0)

    def write(k):
        return pltpu.make_async_copy(last_ref.at[k], out_ref.at[k], out_sem.at[k])

    def back_of(half):
        def back_step(i, carry):
            b = lax.rem(mybin + 4 - lax.div(i, 4), 4)
            q = lax.rem(i, 4)
            k = 8 * lax.rem(myz + lax.div(q, 2), 2) + 4 * lax.rem(myx + q, 2) + b
            eight = pl.ds(pl.multiple_of(8 * k, 8), 8)
            pltpu.make_async_copy(
                ret_ref.at[half, eight], land_ref.at[half, eight], ret_recv.at[half, k]
            ).wait()
            Z = back_matmul(half, k, land_ref, wb_ref)
            if half == 0:
                last_ref[k] = Z
            else:
                back_twiddle(k, last_ref[k] + Z, tw_ref, last_ref)
                write(k).start()
            return carry

        lax.fori_loop(0, 16, back_step, 0)

    back_of(0)
    back_of(1)

    def finish(half, carry):
        for src, sem in ((send_ref, go_send), (ret_ref, ret_send)):
            part = src.at[half, pl.ds(0, DEV - 1)]
            pltpu.make_async_remote_copy(
                src_ref=part, dst_ref=part, send_sem=sem.at[half], recv_sem=sem.at[half],
                device_id=me, device_id_type=FLAT,
            ).wait_send()
        return carry

    lax.fori_loop(0, 2, finish, 0)

    def written(k, carry):
        write(k).wait()
        return carry

    lax.fori_loop(0, 16, written, 0)


def main_stage(g1, g2, weights, tab):
    hbm = pl.BlockSpec(memory_space=pl.ANY)
    return pl.pallas_call(
        main_kernel,
        in_specs=[pl.BlockSpec(memory_space=pltpu.SMEM)] + [hbm] * 7,
        out_specs=hbm,
        out_shape=jax.ShapeDtypeStruct((16, 128, 256), F32),
        scratch_shapes=[
            pltpu.VMEM((A, 2, 8, L), F32),
            pltpu.VMEM((2, 2, 256, 256), BF16),
            pltpu.VMEM((2, 256, 256), BF16),
            pltpu.VMEM((2, 256, 256), BF16),
            pltpu.VMEM((2, 2, 2, 128, 256), BF16),
            pltpu.VMEM((2, 128, N), F32),
            pltpu.VMEM((16, 128, 256), F32),
            pltpu.VMEM((2, DEV, 2, 2, 8, L), F32),
            pltpu.VMEM((2, DEV, 2, 2, 8, L), F32),
            pltpu.VMEM((A, 64, 256), F32),
            pltpu.VMEM((A, 32, 256), F32),
            pltpu.VMEM((2, DEV, 2, 8, L), F32),
            pltpu.VMEM((2, DEV, 2, 8, L), F32),
            pltpu.VMEM((16, 128, 256), F32),
            pltpu.SemaphoreType.DMA((5,)),
            pltpu.SemaphoreType.DMA((2, 4)),
            pltpu.SemaphoreType.DMA((2,)),
            pltpu.SemaphoreType.DMA((2,)),
            pltpu.SemaphoreType.DMA((2,)),
            pltpu.SemaphoreType.DMA((2, 16)),
            pltpu.SemaphoreType.DMA((16,)),
        ],
        compiler_params=pltpu.CompilerParams(
            collective_id=0, has_side_effects=True, vmem_limit_bytes=62 * 2**20
        ),
        name="main",
    )(
        weights, g1.reshape(128, N), g2.reshape(128, N),
        tab["twid"], tab["row"], tab["colf"], tab["coli"], tab["back"],
    )


def last_kernel(z_ref, out_ref):
    for j in range(ROWS // 8):
        rows = slice(8 * j, 8 * j + 8)
        X = [(z_ref[0, rows, 0:L], None)]
        X += [(z_ref[k, rows, 0:L], z_ref[k, rows, L : 2 * L]) for k in range(1, 16)]
        X += [(z_ref[0, rows, L : 2 * L], None)]
        for p, v in enumerate(irfft(X, A)):
            out_ref[rows, L * p : L * p + L] = v


def last_stage(z):
    return pl.pallas_call(
        last_kernel,
        grid=(STEPS,),
        in_specs=[pl.BlockSpec((16, ROWS, 256), lambda i: (0, i, 0))],
        out_specs=pl.BlockSpec((ROWS, N), lambda i: (i, 0)),
        out_shape=jax.ShapeDtypeStruct((128, N), F32),
        name="last",
    )(z)


def on_device(shear_one, shear_two, weights):
    tab = {k: jnp.asarray(v) for k, v in tables().items()}
    z = main_stage(shear_one, shear_two, weights, tab)
    return last_stage(z).reshape(1, 128, N)


def solution(mesh):
    spec = P("bin", "tile", None)
    return jax.shard_map(
        on_device, mesh=mesh, in_specs=(spec, spec, P()), out_specs=spec, check_vma=False
    )
```
